512 devices in a mesh: grp: 8 (over z_lo, x), tile: 64 (over y, z_hi, core).
Axes of the slice: x: 4, y: 8, z: 8 (z_hi: 4, z_lo: 2; z = z_hi * 2 + z_lo), core: 2. Of those that a mesh axis runs over, the one named last changes fastest.
Arguments:
- pixels: bfloat16 [512, 128, 3, 256], P(('grp', 'tile')), parts along dimension 0, may hold values from -6 to 6
- patch_weight: bfloat16 [768, 1024], P('tile'), may hold values from -0.21875 to 0.21875
- qkv_weight: bfloat16 [1024, 1536], P('tile'), may hold values from -2.0625 to 2.0625
- out_weight: bfloat16 [512, 1024], P('tile'), may hold values from -0.25 to 0.25
- reward_head: float32 [1024], replicated, may hold values from -4 to 4
- conv_weight: bfloat16 [3, 3, 48, 3], replicated, may hold values from -1.25 to 1.25
Outputs:
- rewards: float32 [512], P(('grp', 'tile')), parts along dimension 0
- act_grad: bfloat16 [512, 128, 48, 256], P('grp', 'tile'), parts along dimension 0
The draws below stay inside these ranges and needn't reach their ends.
There are 8 independent parts, one for each index of `grp`. The reference program is written for one: setup_inputs(seed, part) draws one part's arguments, and reference() takes and returns one part's arrays. A program takes and returns all parts, laid end to end along the dimension named above; an argument that names none is the same for every part. Nothing has to cross between parts.
All inputs are finite; a program needn't handle non-finite values.
Results may differ from the reference program's by a relative error of at most 0.02.
Values may be sent and summed in bfloat16 or wider, within the bound.
No kernel may reach another device: no remote copies, remote signals or barrier semaphores. Data moves between devices by JAX's collectives and lax.ppermute only.
A program may use at most 64 MiB of HBM per device.

```python
import jax
import jax.numpy as jnp
from jax import lax

D = 1024
HEADS = 8
HEAD_DIM = 64
PATCH = 16
PDIM = 768
C_DEC = 48
W = 256
FRAMES = 64
H = 128


def draw_qkv_weight(key, part):
    inner_width = HEADS * HEAD_DIM
    base = jax.random.truncated_normal(key, -4.0, 4.0, (D, 3 * inner_width), jnp.float32) * D ** (-0.5)
    return base.astype(jnp.bfloat16)


def shard_levels(rng, dims, split, least, top_value):
    gain, own = 1.0, jax.random.fold_in(rng, 6)
    for axis_at, shards_of in split:
        steps = jnp.exp(jax.random.uniform(jax.random.fold_in(own, axis_at), (shards_of,), jnp.float32, least / len(split), top_value / len(split)))
        gain = gain * jnp.repeat(steps, dims[axis_at] // shards_of).reshape([-1 if axis == axis_at else 1 for axis in range(len(dims))])
    return gain


def normal_values(key, extent, deviation, most, shards=(), held_as=jnp.bfloat16):
    array = deviation * jax.random.normal(key, extent, jnp.float32)
    if shards:
        array = array * shard_levels(key, extent, shards, -0.22, 0.18)
    return jnp.clip(array, -most, most).astype(held_as)


def setup_inputs(seed: int = 0, part: int = 0) -> dict:
    keys = jax.random.split(jax.random.key(seed), 7)
    part_keys = jax.random.split(jax.random.fold_in(keys[6], part), 7)
    return {
        "pixels": normal_values(part_keys[0], (FRAMES, H, 3, W), 1.0, 6.0, ((0, 64),)),
        "patch_weight": normal_values(keys[1], (PDIM, D), PDIM ** -0.5, 0.21875, ((0, 64),)),
        "qkv_weight": draw_qkv_weight(jax.random.fold_in(keys[6], 71), part),
        "out_weight": normal_values(keys[3], (HEADS * HEAD_DIM, D), (HEADS * HEAD_DIM) ** -0.5, 0.25, ((0, 64),)),
        "reward_head": normal_values(keys[4], (D,), 0.3, 4.0, (), jnp.float32),
        "conv_weight": normal_values(keys[5], (3, 3, C_DEC, 3), 27 ** -0.5, 1.25),
    }


LOSS_SCALE = 1024.0
NORM_EPSILON = 1e-05

def normalize(values_in):
    average = lax.optimization_barrier(jnp.mean(values_in, -1, keepdims=True))
    centred = values_in - average
    inverse_scale = lax.rsqrt(lax.optimization_barrier(jnp.mean(centred * centred, -1, keepdims=True)) + NORM_EPSILON)
    return (centred * inverse_scale, inverse_scale)

def norm_back(grad_in, normed, inverse_scale):
    return inverse_scale * (grad_in - lax.optimization_barrier(jnp.mean(grad_in, -1, keepdims=True)) - normed * lax.optimization_barrier(jnp.mean(grad_in * normed, -1, keepdims=True)))

def to_patch_rows(pixels):
    frame_count, row_count, _, col_count = pixels.shape
    blocks = pixels.reshape(frame_count, row_count // PATCH, PATCH, 3, col_count // PATCH, PATCH)
    blocks = blocks.transpose(0, 1, 4, 3, 2, 5)
    return blocks.reshape(frame_count, row_count // PATCH * (col_count // PATCH), 3 * PATCH * PATCH)

def from_patch_rows(patches, row_count, col_count):
    frame_count = patches.shape[0]
    blocks = patches.reshape(frame_count, row_count // PATCH, col_count // PATCH, 3, PATCH, PATCH)
    blocks = blocks.transpose(0, 1, 4, 3, 2, 5)
    return blocks.reshape(frame_count, row_count, 3, col_count)

def conv_transpose(padded, conv_weight, row_count, col_count):
    frame_count = padded.shape[0]
    pieces = [padded[:, 2 - row_off:2 - row_off + row_count, :, 2 - col_off:2 - col_off + col_count] for row_off in range(3) for col_off in range(3)]
    stacked = jnp.stack(pieces, 2).reshape(frame_count, row_count, 27, col_count)
    kernel = conv_weight.transpose(0, 1, 3, 2).reshape(27, -1)
    result = jnp.einsum('fykx,kc->fycx', stacked.astype(jnp.float32), kernel.astype(jnp.float32))
    return result.astype(jnp.bfloat16)

def reference(pixels, patch_weight, qkv_weight, out_weight, reward_head, conv_weight):
    frame_count, row_count, _, col_count = pixels.shape
    model_width = patch_weight.shape[1]
    inner_width = out_weight.shape[0]
    score_scale = HEAD_DIM ** (-0.5)
    patches = to_patch_rows(pixels)
    patch_count = patches.shape[1]
    embedded = jnp.dot(patches.reshape(-1, PDIM), patch_weight, preferred_element_type=jnp.float32)
    embedded = embedded.astype(jnp.bfloat16).reshape(frame_count, patch_count, model_width)
    first_normed, first_scale = normalize(embedded.astype(jnp.float32))
    projected = jnp.dot(first_normed.astype(jnp.bfloat16).reshape(-1, model_width), qkv_weight, preferred_element_type=jnp.float32)
    projected = projected.astype(jnp.bfloat16).reshape(frame_count, patch_count, 3, HEADS, HEAD_DIM)
    query_rows = projected[:, :, 0].astype(jnp.float32)
    key_rows = projected[:, :, 1].astype(jnp.float32)
    value_rows = projected[:, :, 2].astype(jnp.float32)
    scores = jnp.einsum('iphd,jphd->phij', query_rows, key_rows) * score_scale
    attn_probs = jax.nn.softmax(scores, axis=-1)
    probs_rounded = attn_probs.astype(jnp.bfloat16).astype(jnp.float32)
    attended = jnp.einsum('phij,jphd->iphd', probs_rounded, value_rows).astype(jnp.bfloat16)
    attended = attended.reshape(frame_count, patch_count, inner_width)
    hidden = embedded.astype(jnp.float32) + jnp.dot(attended.reshape(-1, inner_width), out_weight, preferred_element_type=jnp.float32).reshape(frame_count, patch_count, model_width)
    second_normed, second_scale = normalize(hidden)
    rewards = lax.optimization_barrier(jnp.mean(lax.optimization_barrier(jnp.sum(second_normed * reward_head, -1)), -1))
    frame_coeff = -LOSS_SCALE * jax.nn.sigmoid(-rewards)
    grad_second = frame_coeff[:, None, None] * reward_head / patch_count
    grad_hidden = norm_back(grad_second, second_normed, second_scale)
    hidden_rounded = grad_hidden.astype(jnp.bfloat16)
    grad_attended = jnp.dot(hidden_rounded.reshape(-1, model_width), out_weight.T, preferred_element_type=jnp.float32)
    grad_attended = grad_attended.astype(jnp.bfloat16).reshape(frame_count, patch_count, HEADS, HEAD_DIM).astype(jnp.float32)
    grad_probs = jnp.einsum('iphd,jphd->phij', grad_attended, value_rows)
    grad_value = jnp.einsum('phij,iphd->jphd', probs_rounded, grad_attended).astype(jnp.bfloat16)
    row_delta = lax.optimization_barrier(jnp.sum(attn_probs * grad_probs, -1, keepdims=True))
    grad_scores = (attn_probs * (grad_probs - row_delta) * score_scale).astype(jnp.bfloat16).astype(jnp.float32)
    grad_query = jnp.einsum('phij,jphd->iphd', grad_scores, key_rows).astype(jnp.bfloat16)
    grad_key = jnp.einsum('phij,iphd->jphd', grad_scores, query_rows).astype(jnp.bfloat16)
    grad_proj = jnp.stack([grad_query, grad_key, grad_value], 2).reshape(-1, 3 * inner_width)
    grad_first = jnp.dot(grad_proj, qkv_weight.T, preferred_element_type=jnp.float32)
    grad_first = grad_first.reshape(frame_count, patch_count, model_width)
    grad_embed = norm_back(grad_first, first_normed, first_scale).astype(jnp.bfloat16)
    grad_total = (grad_hidden + grad_embed.astype(jnp.float32)).astype(jnp.bfloat16)
    grad_patches = jnp.dot(grad_total.reshape(-1, model_width), patch_weight.T, preferred_element_type=jnp.float32)
    grad_patches = grad_patches.astype(jnp.bfloat16).reshape(frame_count, patch_count, PDIM)
    grad_pixels = from_patch_rows(grad_patches, row_count, col_count)
    padded = jnp.pad(grad_pixels, ((0, 0), (1, 1), (0, 0), (1, 1)))
    act_grad = conv_transpose(padded, conv_weight, row_count, col_count)
    return (rewards, act_grad)
```

```python
import jax
import jax.numpy as jnp
from jax import lax
from jax.sharding import Mesh
from jax.sharding import PartitionSpec as P

D = 1024
HEADS = 8
HEAD_DIM = 64
PATCH = 16
PDIM = 768


GRP = ("zl", "x")
TILE = ("y", "zh", "core")
ROW = ("zh", "core")

LOSS_SCALE = 1024.0
NORM_EPSILON = 1e-05


def extended(value, sides, width):
    for axis, dim in sides:
        devices, length = (lax.axis_size(axis), value.shape[dim])
        up = [(i, (i + 1) % devices) for i in range(devices - 1)]
        down = [(j, i) for i, j in up]
        last = lax.slice_in_dim(value, length - width, length, axis=dim)
        first = lax.slice_in_dim(value, 0, width, axis=dim)
        before = lax.ppermute(last, axis, up)
        after = lax.ppermute(first, axis, down)
        value = jnp.concatenate([before, value, after], axis=dim)
    return value


def normalize(values_in):
    average = jnp.mean(values_in, -1, keepdims=True)
    centred = values_in - average
    inverse_scale = lax.rsqrt(jnp.mean(centred * centred, -1, keepdims=True) + NORM_EPSILON)
    return (centred * inverse_scale, inverse_scale)


def norm_back(grad_in, normed, inverse_scale):
    return inverse_scale * (
        grad_in
        - jnp.mean(grad_in, -1, keepdims=True)
        - normed * jnp.mean(grad_in * normed, -1, keepdims=True)
    )


def to_patch_rows(pixels):
    frame_count, row_count, _, col_count = pixels.shape
    blocks = pixels.reshape(frame_count, row_count // PATCH, PATCH, 3, col_count // PATCH, PATCH)
    blocks = blocks.transpose(0, 1, 4, 3, 2, 5)
    return blocks.reshape(frame_count, row_count // PATCH * (col_count // PATCH), 3 * PATCH * PATCH)


def from_patch_rows(patches, row_count, col_count):
    frame_count = patches.shape[0]
    blocks = patches.reshape(frame_count, row_count // PATCH, col_count // PATCH, 3, PATCH, PATCH)
    blocks = blocks.transpose(0, 1, 4, 3, 2, 5)
    return blocks.reshape(frame_count, row_count, 3, col_count)


def attend_forward(spread, full_qkv):
    frame_count, local_count, model_width = spread.shape
    score_scale = HEAD_DIM ** (-0.5)
    first_normed, first_scale = normalize(spread.astype(jnp.float32))
    projected = jnp.dot(
        first_normed.astype(jnp.bfloat16).reshape(-1, model_width),
        full_qkv,
        preferred_element_type=jnp.float32,
    )
    projected = projected.astype(jnp.bfloat16).reshape(frame_count, local_count, 3, HEADS, HEAD_DIM)
    query_rows = projected[:, :, 0]
    key_rows = projected[:, :, 1]
    value_rows = projected[:, :, 2]
    scores = (
        jnp.einsum("iphd,jphd->phij", query_rows, key_rows, preferred_element_type=jnp.float32)
        * score_scale
    )
    attn_probs = jax.nn.softmax(scores, axis=-1)
    probs_rounded = attn_probs.astype(jnp.bfloat16)
    attended = jnp.einsum(
        "phij,jphd->iphd", probs_rounded, value_rows, preferred_element_type=jnp.float32
    )
    attended = attended.astype(jnp.bfloat16).reshape(frame_count, local_count, HEADS * HEAD_DIM)
    return (
        first_normed,
        first_scale,
        query_rows,
        key_rows,
        value_rows,
        attn_probs,
        probs_rounded,
        attended,
    )


def attend_backward(grad_spread, saved, back_qkv):
    first_normed, first_scale, query_rows, key_rows, value_rows, attn_probs, probs_rounded, _ = (
        saved
    )
    frame_count, local_count = (first_normed.shape[0], first_normed.shape[1])
    score_scale = HEAD_DIM ** (-0.5)
    grad_heads = grad_spread.reshape(frame_count, local_count, HEADS, HEAD_DIM)
    grad_probs = jnp.einsum(
        "iphd,jphd->phij", grad_heads, value_rows, preferred_element_type=jnp.float32
    )
    grad_value = jnp.einsum(
        "phij,iphd->jphd", probs_rounded, grad_heads, preferred_element_type=jnp.float32
    ).astype(jnp.bfloat16)
    row_delta = jnp.sum(attn_probs * grad_probs, -1, keepdims=True)
    grad_scores = (attn_probs * (grad_probs - row_delta) * score_scale).astype(jnp.bfloat16)
    grad_query = jnp.einsum(
        "phij,jphd->iphd", grad_scores, key_rows, preferred_element_type=jnp.float32
    ).astype(jnp.bfloat16)
    grad_key = jnp.einsum(
        "phij,iphd->jphd", grad_scores, query_rows, preferred_element_type=jnp.float32
    ).astype(jnp.bfloat16)
    grad_proj = jnp.stack([grad_query, grad_key, grad_value], 2).reshape(-1, 3 * HEADS * HEAD_DIM)
    grad_first = jnp.dot(grad_proj, back_qkv.T, preferred_element_type=jnp.float32)
    grad_first = grad_first.reshape(first_normed.shape)
    return norm_back(grad_first, first_normed, first_scale).astype(jnp.bfloat16)


def gather_weights(patch_weight, qkv_weight, out_weight):
    half = out_weight.shape[1] // 2
    rows = qkv_weight.shape[0]
    packed = jnp.concatenate(
        [
            jnp.pad(patch_weight, ((0, rows - patch_weight.shape[0]), (0, 0))),
            qkv_weight,
            jnp.concatenate([out_weight[:, :half], out_weight[:, half:]], 0),
        ],
        1,
    )
    full = lax.all_gather(packed, TILE, axis=0, tiled=True)
    width = patch_weight.shape[1]
    inner = qkv_weight.shape[1]
    full_patch = full[:, :width].reshape(-1, rows, width)[:, : patch_weight.shape[0]]
    full_qkv = full[:, width : width + inner]
    full_out = full[:, width + inner :].reshape(-1, 2, out_weight.shape[0], half)
    full_out = full_out.transpose(0, 2, 1, 3)
    return full_patch.reshape(-1, width), full_qkv, full_out.reshape(-1, 2 * half)


def on_device(pixels, patch_weight, qkv_weight, out_weight, reward_head, conv_weight):
    local_frames, row_count, _, col_count = pixels.shape
    model_width = D
    inner_width = HEADS * HEAD_DIM
    full_patch, full_qkv, full_out = gather_weights(patch_weight, qkv_weight, out_weight)
    patches = to_patch_rows(pixels)
    patch_count = patches.shape[1]
    spread_patches = lax.all_to_all(patches, TILE, split_axis=1, concat_axis=0, tiled=True)
    frame_count, local_count = (spread_patches.shape[0], spread_patches.shape[1])
    embedded = jnp.dot(
        spread_patches.reshape(-1, PDIM), full_patch, preferred_element_type=jnp.float32
    )
    embedded = embedded.astype(jnp.bfloat16).reshape(frame_count, local_count, model_width)
    saved = attend_forward(embedded, full_qkv)
    hidden = embedded.astype(jnp.float32) + jnp.dot(
        saved[7].reshape(-1, inner_width), full_out, preferred_element_type=jnp.float32
    ).reshape(embedded.shape)
    second_normed, second_scale = normalize(hidden)
    partial_sums = jnp.sum(jnp.sum(second_normed * reward_head, -1), -1)
    copies = jnp.broadcast_to(partial_sums, (frame_count // local_frames, frame_count))
    everyone = lax.all_to_all(copies, TILE, split_axis=0, concat_axis=0, tiled=True)
    all_rewards = jnp.sum(everyone, 0) / patch_count
    rewards = lax.dynamic_slice_in_dim(
        all_rewards, lax.axis_index(TILE) * local_frames, local_frames
    )
    frame_coeff = -LOSS_SCALE * jax.nn.sigmoid(-all_rewards)
    grad_second = frame_coeff[:, None, None] * reward_head / patch_count
    grad_hidden = norm_back(grad_second, second_normed, second_scale)
    hidden_rounded = grad_hidden.astype(jnp.bfloat16)
    grad_attended = jnp.dot(
        hidden_rounded.reshape(-1, model_width), full_out.T, preferred_element_type=jnp.float32
    )
    grad_attended = grad_attended.astype(jnp.bfloat16).reshape(
        hidden.shape[0], hidden.shape[1], inner_width
    )
    grad_embed = attend_backward(grad_attended, saved, full_qkv)
    grad_total = (grad_hidden + grad_embed.astype(jnp.float32)).astype(jnp.bfloat16)
    grad_patches = jnp.dot(
        grad_total.reshape(-1, model_width), full_patch.T, preferred_element_type=jnp.float32
    )
    sharers = lax.axis_size(ROW)
    tile_rows = PATCH // sharers
    grad_rows = grad_patches.astype(jnp.bfloat16).reshape(
        frame_count, local_count, 3, sharers, tile_rows, PATCH
    )
    grad_rows = grad_rows.transpose(3, 0, 4, 2, 1, 5).reshape(
        sharers, frame_count, tile_rows, 3, local_count * PATCH
    )
    row_grad = lax.all_to_all(grad_rows, ROW, split_axis=0, concat_axis=0, tiled=True)
    row_grad = row_grad.transpose(1, 2, 3, 0, 4).reshape(frame_count, tile_rows, 3, col_count)
    padded = extended(row_grad, ((TILE, 1),), 1)
    padded = jnp.pad(padded, ((0, 0), (0, 0), (0, 0), (1, 1)))
    pieces = [
        padded[:, 2 - row_off : 2 - row_off + tile_rows, :, 2 - col_off : 2 - col_off + col_count]
        for row_off in range(3)
        for col_off in range(3)
    ]
    stacked = jnp.stack(pieces, 2).reshape(row_grad.shape[0], tile_rows, 27, col_count)
    kernel = conv_weight.transpose(0, 1, 3, 2).reshape(27, -1)
    act_grad = jnp.einsum(
        "fykx,kc->fycx", stacked, kernel, preferred_element_type=jnp.float32
    ).astype(jnp.bfloat16)
    return (rewards, act_grad)


def solution(mesh):
    axes = Mesh(mesh.devices.reshape(2, 4, 8, 4, 2), GRP + TILE)
    in_specs = (
        P(GRP + TILE, None, None, None),
        P(TILE, None),
        P(TILE, None),
        P(TILE, None),
        P(),
        P(),
    )
    out_specs = (P(GRP + TILE), P(GRP, TILE, None, None))
    return jax.shard_map(
        on_device, mesh=axes, in_specs=in_specs, out_specs=out_specs, check_vma=False
    )
```

```python
import jax
import jax.numpy as jnp
from jax import lax
from jax.experimental import pallas as pl
from jax.experimental.pallas import tpu as pltpu
from jax.sharding import Mesh
from jax.sharding import PartitionSpec as P

D = 1024
HEADS = 8
HEAD_DIM = 64
PATCH = 16
PDIM = 768
INNER = HEADS * HEAD_DIM
SLOT = 16
PADDED = 1024
FRAMES = 64
PATCHES = 128
ROWS = 128
IMAGE_W = 256

GRP = ("zl", "x")
TILE = ("y", "zh", "core")
ROW = ("zh", "core")

LOSS_SCALE = 1024.0
NORM_EPSILON = 1e-05
F32 = jnp.float32
BF16 = jnp.bfloat16


def iota(shape, dim):
    return lax.broadcasted_iota(jnp.int32, shape, dim)


def dot(a, b):
    return lax.dot_general(a, b, (((1,), (0,)), ((), ())), preferred_element_type=F32)


def dot_t(a, b):
    return lax.dot_general(a, b, (((1,), (1,)), ((), ())), preferred_element_type=F32)


def t_dot(a, b):
    return lax.dot_general(a, b, (((0,), (0,)), ((), ())), preferred_element_type=F32)


def one_hot(condition):
    return jnp.where(condition, 1.0, 0.0).astype(F32).astype(BF16)


def normalize(values_in):
    centred = values_in - jnp.mean(values_in, -1, keepdims=True)
    inverse_scale = lax.rsqrt(jnp.mean(centred * centred, -1, keepdims=True) + NORM_EPSILON)
    return centred * inverse_scale, inverse_scale


def norm_back(grad_in, normed, inverse_scale):
    return inverse_scale * (
        grad_in
        - jnp.mean(grad_in, -1, keepdims=True)
        - normed * jnp.mean(grad_in * normed, -1, keepdims=True)
    )


def weight_copies(packed, target, sems, first, low, width):
    copies = []
    for core in range(2):
        for zh in range(4):
            copies.append(
                pltpu.make_async_copy(
                    packed.at[:, core, zh, :, pl.ds(low, width)],
                    target.at[:, zh, core],
                    sems.at[first + core * 4 + zh],
                )
            )
    return copies


def start_all(copies):
    for copy in copies:
        copy.start()


def wait_all(copies):
    for copy in copies:
        copy.wait()


def spread_kernel(patches_ref, out_ref, select_ref):
    to_row = iota((ROWS, ROWS), 0)
    from_row = iota((ROWS, ROWS), 1)
    order = one_hot(from_row == 2 * (to_row & (FRAMES - 1)) + (to_row >> 6))
    ordered = dot(order, patches_ref[...]).astype(BF16)
    slot = iota((PDIM, PADDED), 1)
    place = one_hot(
        ((slot & 15) < 12) & (iota((PDIM, PADDED), 0) == 12 * (slot >> 4) + (slot & 15))
    )
    out_ref[...] = dot(ordered, place).astype(BF16)
    slot = iota((PDIM, PADDED), 1)
    value = 12 * (slot >> 4) + (slot & 15)
    row = (value >> 4) & 15
    target = (row >> 1) * 96 + (row & 1) * 48 + (value >> 8) * 16 + (value & 15)
    select_ref[...] = one_hot(((slot & 15) < 12) & (iota((PDIM, PADDED), 0) == target))


def half_mask():
    return iota((ROWS, 2 * HEAD_DIM), 1) < HEAD_DIM


def pick(condition, value):
    return jnp.where(condition, value.astype(F32), 0.0).astype(BF16)


def forward_kernel(
    patches_ref,
    packed_ref,
    head_ref,
    normed_ref,
    scale_ref,
    proj_ref,
    probs_ref,
    second_ref,
    second_scale_ref,
    out_weight_ref,
    sums_ref,
    patch_w,
    qkv_w,
    out_w,
    sems,
):
    patch_copies = weight_copies(packed_ref, patch_w, sems, 0, 0, D)
    qkv_copies = weight_copies(packed_ref, qkv_w, sems, 8, D, 3 * INNER)
    out_copies = weight_copies(packed_ref, out_w, sems, 16, D + 3 * INNER, D // 2)
    start_all(patch_copies + qkv_copies + out_copies)
    wait_all(patch_copies)
    embedded = dot(patches_ref[...], patch_w[...].reshape(PADDED, D)).astype(BF16).astype(F32)
    normed, scale = normalize(embedded)
    normed_ref[...] = normed
    scale_ref[...] = jnp.broadcast_to(scale, (ROWS, 128))
    wait_all(qkv_copies)
    proj_ref[...] = dot(normed.astype(BF16), qkv_w[...].reshape(D, 3 * INNER)).astype(BF16)
    wait_all(out_copies)
    halves = out_w[...].reshape(64, SLOT, D // 2).astype(F32).reshape(64, 2, SLOT // 2, D // 2)
    for half in range(2):
        out_weight_ref[:, half * (D // 2) : (half + 1) * (D // 2)] = (
            halves[:, half].reshape(INNER, D // 2).astype(BF16)
        )
    same_patch = (iota((ROWS, ROWS), 0) >> 6) == (iota((ROWS, ROWS), 1) >> 6)
    low = half_mask()
    attended = []
    for pair in range(HEADS // 2):
        at = pair * 2 * HEAD_DIM
        query = proj_ref[:, at : at + 128]
        key = proj_ref[:, INNER + at : INNER + at + 128]
        value = proj_ref[:, 2 * INNER + at : 2 * INNER + at + 128]
        parts = []
        for side in range(2):
            mine = low if side == 0 else jnp.logical_not(low)
            scores = dot_t(pick(mine, query), key) * HEAD_DIM ** (-0.5)
            scores = jnp.where(same_patch, scores, -1e30)
            weights = jnp.exp(scores - jnp.max(scores, -1, keepdims=True))
            probs = weights / jnp.sum(weights, -1, keepdims=True)
            probs_ref[2 * pair + side] = probs
            parts.append(dot(probs.astype(BF16), value))
        attended.append(jnp.where(low, parts[0], parts[1]).astype(BF16))
    hidden = embedded + dot(jnp.concatenate(attended, 1), out_weight_ref[...])
    second, second_scale = normalize(hidden)
    second_ref[...] = second
    second_scale_ref[...] = jnp.broadcast_to(second_scale, (ROWS, 128))
    column = jnp.sum(second * head_ref[0:1, :], -1, keepdims=True)
    on_diagonal = iota((ROWS, ROWS), 0) == iota((ROWS, ROWS), 1)
    line = jnp.sum(jnp.where(on_diagonal, column, 0.0), 0, keepdims=True)
    sums_ref[...] = jnp.broadcast_to(line, (64, ROWS))


def before_kernel(
    second_ref,
    second_scale_ref,
    head_ref,
    out_weight_ref,
    proj_ref,
    probs_ref,
    select_ref,
    packed_ref,
    hidden_ref,
    attended_ref,
    scores_ref,
    back_ref,
    patch_w,
    sems,
):
    patch_copies = weight_copies(packed_ref, patch_w, sems, 0, 0, D)
    start_all(patch_copies)
    second = second_ref[...]
    direction = head_ref[0:1, :] / PATCHES
    hidden = norm_back(direction, second, second_scale_ref[:, 0:1])
    hidden_ref[...] = hidden
    grad_attended = dot_t(hidden.astype(BF16), out_weight_ref[...])
    attended_ref[...] = grad_attended
    low = half_mask()
    for pair in range(HEADS // 2):
        at = pair * 2 * HEAD_DIM
        value = proj_ref[:, 2 * INNER + at : 2 * INNER + at + 128]
        grad = grad_attended[:, at : at + 128]
        for side in range(2):
            mine = low if side == 0 else jnp.logical_not(low)
            grad_probs = dot_t(pick(mine, grad), value)
            probs = probs_ref[2 * pair + side]
            delta = jnp.sum(probs * grad_probs, -1, keepdims=True)
            scores_ref[2 * pair + side] = probs * (grad_probs - delta) * HEAD_DIM ** (-0.5)
    wait_all(patch_copies)
    back_ref[...] = dot(select_ref[...], patch_w[...].reshape(PADDED, D)).astype(BF16)


def backward_kernel(
    everyone_ref,
    scores_ref,
    attended_ref,
    hidden_ref,
    proj_ref,
    probs_ref,
    normed_ref,
    scale_ref,
    back_ref,
    packed_ref,
    grad_ref,
    rewards_ref,
    grad_proj,
    qkv_w,
    sems,
):
    qkv_copies = weight_copies(packed_ref, qkv_w, sems, 0, D, 3 * INNER)
    start_all(qkv_copies)
    total = jnp.sum(everyone_ref[...], 0, keepdims=True)
    same_frame = (iota((ROWS, ROWS), 0) & 63) == (iota((ROWS, ROWS), 1) & 63)
    rewards = jnp.sum(jnp.where(same_frame, total, 0.0), 1, keepdims=True) / PATCHES
    factor = -LOSS_SCALE / (1.0 + jnp.exp(rewards))
    on_diagonal = iota((ROWS, ROWS), 0) == iota((ROWS, ROWS), 1)
    line = jnp.sum(jnp.where(on_diagonal, rewards, 0.0), 0, keepdims=True)
    rewards_ref[...] = jnp.broadcast_to(line, (8, ROWS))
    low = half_mask()
    for pair in range(HEADS // 2):
        at = pair * 2 * HEAD_DIM
        query = proj_ref[:, at : at + 128]
        key = proj_ref[:, INNER + at : INNER + at + 128]
        grad = (factor * attended_ref[:, at : at + 128]).astype(BF16)
        parts = []
        for side in range(2):
            scores = (factor * scores_ref[2 * pair + side]).astype(BF16)
            probs = probs_ref[2 * pair + side].astype(BF16)
            parts.append((dot(scores, key), t_dot(scores, query), t_dot(probs, grad)))
        for part in range(3):
            grad_proj[:, part * INNER + at : part * INNER + at + 128] = jnp.where(
                low, parts[0][part], parts[1][part]
            ).astype(BF16)
    wait_all(qkv_copies)
    grad_first = dot_t(grad_proj[...], qkv_w[...].reshape(D, 3 * INNER))
    grad_embed = norm_back(grad_first, normed_ref[...], scale_ref[:, 0:1]).astype(BF16)
    grad_total = (factor * hidden_ref[...] + grad_embed.astype(F32)).astype(BF16)
    grad_ref[...] = dot_t(back_ref[...], grad_total).astype(BF16)


def conv_kernel(rows_ref, kernel_ref, out_ref):
    frames = rows_ref.shape[0]
    kernel = kernel_ref[...]
    lane = iota((16, IMAGE_W), 1)
    for frame in range(frames):
        rows = rows_ref[frame].astype(F32)
        right = jnp.where(lane == IMAGE_W - 1, 0.0, pltpu.roll(rows, IMAGE_W - 1, 1))
        left = jnp.where(lane == 0, 0.0, pltpu.roll(rows, 1, 1))
        taps = jnp.concatenate([right, rows, left], 0).astype(BF16)
        result = dot(kernel, taps).astype(BF16)
        for row in range(2):
            out_ref[frame, row] = result[row * 48 : (row + 1) * 48]


def shape(dims, dtype):
    return jax.ShapeDtypeStruct(dims, dtype)


def vmem(count):
    return [pl.BlockSpec(memory_space=pltpu.VMEM)] * count


ANYWHERE = pl.BlockSpec(memory_space=pl.ANY)
WEIGHT = (8, 4, 2, SLOT)


def to_patch_rows(pixels):
    frame_count, row_count, _, col_count = pixels.shape
    blocks = pixels.reshape(frame_count, row_count // PATCH, PATCH, 3, col_count // PATCH, PATCH)
    blocks = blocks.transpose(0, 1, 4, 3, 2, 5)
    return blocks.reshape(frame_count, row_count // PATCH * (col_count // PATCH), 3 * PATCH * PATCH)


def conv_matrix(conv_weight):
    flipped = conv_weight[::-1]
    per_row = jnp.stack(
        [jnp.pad(flipped, ((y, 1 - y), (0, 0), (0, 0), (0, 0))) for y in range(2)], 0
    )
    matrix = per_row.transpose(0, 3, 2, 1, 4).reshape(-1, 3, 12)
    return jnp.pad(matrix, ((0, 0), (0, 0), (0, 4))).reshape(-1, 48)


def gather_weights(patch_weight, qkv_weight, out_weight):
    half = out_weight.shape[1] // 2
    packed = jnp.concatenate(
        [
            jnp.pad(patch_weight, ((0, SLOT - patch_weight.shape[0]), (0, 0))),
            qkv_weight,
            jnp.concatenate([out_weight[:, :half], out_weight[:, half:]], 0),
        ],
        1,
    )
    return lax.all_gather(packed, "zh", axis=0)


def on_device(pixels, patch_weight, qkv_weight, out_weight, reward_head, conv_weight):
    near = gather_weights(patch_weight, qkv_weight, out_weight)
    near, pixels, conv_weight = lax.optimization_barrier((near, pixels, conv_weight))
    packed = lax.all_gather(near, ("y", "core"), axis=0)
    packed = packed.reshape(8, 2, 4, SLOT, packed.shape[-1])
    patches = to_patch_rows(pixels)
    spread = lax.all_to_all(patches, TILE, split_axis=1, concat_axis=0, tiled=True)
    spread, matrix = lax.optimization_barrier((spread, conv_matrix(conv_weight)))
    head = jnp.broadcast_to(reward_head[None], (8, D))
    slots, select = pl.pallas_call(
        spread_kernel,
        out_shape=(shape((ROWS, PADDED), BF16), shape((PDIM, PADDED), BF16)),
        name="spread",
    )(spread.reshape(ROWS, PDIM))
    normed, scale, proj, probs, second, second_scale, out_full, sums = pl.pallas_call(
        forward_kernel,
        out_shape=(
            shape((ROWS, D), F32),
            shape((ROWS, 128), F32),
            shape((ROWS, 3 * INNER), BF16),
            shape((HEADS, ROWS, ROWS), F32),
            shape((ROWS, D), F32),
            shape((ROWS, 128), F32),
            shape((INNER, D), BF16),
            shape((64, ROWS), F32),
        ),
        in_specs=vmem(1) + [ANYWHERE] + vmem(1),
        out_specs=tuple(vmem(8)),
        scratch_shapes=[
            pltpu.VMEM(WEIGHT + (D,), BF16),
            pltpu.VMEM(WEIGHT + (3 * INNER,), BF16),
            pltpu.VMEM(WEIGHT + (D // 2,), BF16),
            pltpu.SemaphoreType.DMA((24,)),
        ],
        name="forward",
    )(slots, packed, head)
    everyone = lax.all_to_all(sums, TILE, split_axis=0, concat_axis=0, tiled=True)
    hidden, attended, scores, back = pl.pallas_call(
        before_kernel,
        out_shape=(
            shape((ROWS, D), F32),
            shape((ROWS, INNER), F32),
            shape((HEADS, ROWS, ROWS), F32),
            shape((PDIM, D), BF16),
        ),
        in_specs=vmem(7) + [ANYWHERE],
        out_specs=tuple(vmem(4)),
        scratch_shapes=[pltpu.VMEM(WEIGHT + (D,), BF16), pltpu.SemaphoreType.DMA((8,))],
        cost_estimate=pl.CostEstimate(flops=2**31, transcendentals=0, bytes_accessed=2**23),
        name="before",
    )(second, second_scale, head, out_full, proj, probs, select, packed)
    grad, rewards = pl.pallas_call(
        backward_kernel,
        out_shape=(shape((PDIM, ROWS), BF16), shape((8, ROWS), F32)),
        in_specs=vmem(9) + [ANYWHERE],
        out_specs=tuple(vmem(2)),
        scratch_shapes=[
            pltpu.VMEM((ROWS, 3 * INNER), BF16),
            pltpu.VMEM(WEIGHT + (3 * INNER,), BF16),
            pltpu.SemaphoreType.DMA((8,)),
        ],
        name="backward",
    )(everyone, scores, attended, hidden, proj, probs, normed, scale, back, packed)
    row_grad = lax.all_to_all(
        grad.reshape(8, PDIM // 8, ROWS), ROW, split_axis=0, concat_axis=0, tiled=True
    )
    row_grad = row_grad.reshape(8, 2, 3 * PATCH, ROWS)
    devices = lax.axis_size(TILE)
    up = [(i, i + 1) for i in range(devices - 1)]
    down = [(i + 1, i) for i in range(devices - 1)]
    before = lax.ppermute(row_grad[:, 1], TILE, up)
    after = lax.ppermute(row_grad[:, 0], TILE, down)
    rows = jnp.concatenate([before[:, None], row_grad, after[:, None]], 1)
    rows = rows.reshape(8, 4, 3, PATCH, 2, FRAMES).transpose(5, 1, 2, 0, 4, 3)
    rows = jnp.pad(rows.reshape(FRAMES, 12, IMAGE_W), ((0, 0), (0, 4), (0, 0)))
    step = 8
    act_grad = pl.pallas_call(
        conv_kernel,
        out_shape=shape((FRAMES, 2, 48, IMAGE_W), BF16),
        grid=(FRAMES // step,),
        in_specs=[
            pl.BlockSpec((step, 16, IMAGE_W), lambda i: (i, 0, 0)),
            pl.BlockSpec((96, 48), lambda i: (0, 0)),
        ],
        out_specs=pl.BlockSpec((step, 2, 48, IMAGE_W), lambda i: (i, 0, 0, 0)),
        name="conv",
    )(rows, matrix)
    mine = lax.dynamic_slice_in_dim(rewards[0], lax.axis_index(TILE), 1)
    return (mine, act_grad)


def solution(mesh):
    axes = Mesh(mesh.devices.reshape(-1, 4, 8, 4, 2), GRP + TILE)
    in_specs = (
        P(GRP + TILE, None, None, None),
        P(TILE, None),
        P(TILE, None),
        P(TILE, None),
        P(),
        P(),
    )
    out_specs = (P(GRP + TILE), P(GRP, TILE, None, None))
    return jax.shard_map(
        on_device, mesh=axes, in_specs=in_specs, out_specs=out_specs, check_vma=False
    )
```

```python
import jax
import jax.numpy as jnp
from jax import lax
from jax.experimental import pallas as pl
from jax.experimental.pallas import tpu as pltpu
from jax.sharding import Mesh
from jax.sharding import PartitionSpec as P

D = 1024
HEADS = 8
HEAD_DIM = 64
PATCH = 16
PDIM = 768
INNER = HEADS * HEAD_DIM
SLOT = 16
SHARE = 12
PATCH_AT, QKV_AT, TAIL_AT, OUT_AT, BLOCK = 0, 48, 112, 144, 176
FRAMES = 64
PATCHES = 128
ROWS = 128
IMAGE_W = 256
TOGETHER = 4
MIB = 2**20

GRP = ("zl", "x")
TILE = ("y", "zh", "core")
ROW = ("zh", "core")

LOSS_SCALE = 1024.0
NORM_EPSILON = 1e-05
F32 = jnp.float32
BF16 = jnp.bfloat16


def iota(shape, dim):
    return lax.broadcasted_iota(jnp.int32, shape, dim)


def dot(a, b):
    return lax.dot_general(a, b, (((1,), (0,)), ((), ())), preferred_element_type=F32)


def dot_t(a, b):
    return lax.dot_general(a, b, (((1,), (1,)), ((), ())), preferred_element_type=F32)


def one_hot(condition):
    return jnp.where(condition, 1.0, 0.0).astype(F32).astype(BF16)


def normalize(values_in):
    centred = values_in - jnp.mean(values_in, -1, keepdims=True)
    inverse_scale = lax.rsqrt(jnp.mean(centred * centred, -1, keepdims=True) + NORM_EPSILON)
    return centred * inverse_scale, inverse_scale


def norm_back(grad_in, normed, inverse_scale):
    return inverse_scale * (
        grad_in
        - jnp.mean(grad_in, -1, keepdims=True)
        - normed * jnp.mean(grad_in * normed, -1, keepdims=True)
    )


def weight_copies(packed, sems, moves):
    copies = []
    for row, rows, column, columns, target in moves:
        for part in range(4):
            copies.append(
                pltpu.make_async_copy(
                    packed.at[4 * part : 4 * part + 4, row : row + rows, column : column + columns],
                    target(slice(4 * part, 4 * part + 4)),
                    sems.at[len(copies)],
                )
            )
    return copies


def qkv_moves(target, low, high):
    head, tail = D - low, high - D
    return [
        (QKV_AT, 64, low, head, lambda part: target.at[part, :, 0:head]),
        (TAIL_AT, 32, 0, tail, lambda part: target.at[part, 0:32, head : head + tail]),
        (TAIL_AT, 32, tail, tail, lambda part: target.at[part, 32:64, head : head + tail]),
    ]


def start_all(copies):
    for copy in copies:
        copy.start()


def wait_all(copies):
    for copy in copies:
        copy.wait()


def arrange_kernel(core_ref, near_ref, out_ref):
    slots = near_ref[pl.ds(4 * core_ref[0], 4)].reshape(4 * SLOT, 3 * D)
    slot = iota((48, 4 * SLOT), 1)
    row = jnp.where((slot & 15) < SHARE, SHARE * (slot >> 4) + (slot & 15), -1)
    take = one_hot(row == iota((48, 4 * SLOT), 0))
    out_ref[PATCH_AT:QKV_AT] = dot(take, slots[:, 0:D]).astype(BF16)
    out_ref[QKV_AT:TAIL_AT] = slots[:, D : 2 * D]
    out_ref[TAIL_AT:OUT_AT, 0:INNER] = slots[0:32, 2 * D : 2 * D + INNER]
    out_ref[TAIL_AT:OUT_AT, INNER:D] = slots[32:64, 2 * D : 2 * D + INNER]
    slot = iota((32, 4 * SLOT), 1)
    for half in range(2):
        row = jnp.where(((slot >> 3) & 1) == half, 8 * (slot >> 4) + (slot & 7), -1)
        take = one_hot(row == iota((32, 4 * SLOT), 0))
        out_ref[OUT_AT:BLOCK, half * INNER : (half + 1) * INNER] = dot(
            take, slots[:, 2 * D + INNER : 3 * D]
        ).astype(BF16)


def spread_kernel(patches_ref, out_ref):
    to_row = iota((ROWS, ROWS), 0)
    order = one_hot(iota((ROWS, ROWS), 1) == 2 * (to_row & (FRAMES - 1)) + (to_row >> 6))
    out_ref[...] = dot(order, patches_ref[...]).astype(BF16)


def half_mask():
    return iota((ROWS, 2 * HEAD_DIM), 1) < HEAD_DIM


def pick(condition, value):
    return jnp.where(condition, value.astype(F32), 0.0).astype(BF16)


def forward_kernel(
    patches_ref,
    packed_ref,
    head_ref,
    normed_out,
    scale_out,
    proj_out,
    probs_out,
    second_out,
    second_scale_out,
    sums_ref,
    patch_w,
    qkv_w,
    out_w,
    normed_ref,
    scale_ref,
    proj_ref,
    probs_ref,
    second_ref,
    second_scale_ref,
    patch_sems,
    qkv_sems,
    weight_sems,
    out_sems,
):
    results = [
        pltpu.make_async_copy(source, target, out_sems.at[i])
        for i, (source, target) in enumerate(
            [
                (normed_ref, normed_out),
                (scale_ref, scale_out),
                (proj_ref, proj_out),
                (second_ref, second_out),
                (second_scale_ref, second_scale_out),
            ]
            + [(probs_ref.at[2 * i : 2 * i + 2], probs_out.at[2 * i : 2 * i + 2]) for i in range(4)]
        )
    ]
    patch_copies = weight_copies(
        packed_ref, patch_sems, [(PATCH_AT, 48, 0, D, lambda part: patch_w.at[part])]
    )
    qkv_copies = weight_copies(packed_ref, qkv_sems, qkv_moves(qkv_w, 0, 3 * INNER))
    out_copies = weight_copies(
        packed_ref, weight_sems, [(OUT_AT, 32, 0, D, lambda part: out_w.at[part])]
    )
    start_all(patch_copies + qkv_copies + out_copies)
    wait_all(patch_copies)
    embedded = dot(patches_ref[...], patch_w[...].reshape(PDIM, D)).astype(BF16).astype(F32)
    normed, scale = normalize(embedded)
    normed_ref[...] = normed
    scale_ref[...] = jnp.broadcast_to(scale, (ROWS, 128))
    start_all(results[0:2])
    wait_all(qkv_copies)
    proj_ref[...] = dot(normed.astype(BF16), qkv_w[...].reshape(D, 3 * INNER)).astype(BF16)
    start_all(results[2:3])
    same_patch = (iota((ROWS, ROWS), 0) >> 6) == (iota((ROWS, ROWS), 1) >> 6)
    low = half_mask()
    attended = []
    for pair in range(HEADS // 2):
        at = pair * 2 * HEAD_DIM
        query = proj_ref[:, at : at + 128]
        key = proj_ref[:, INNER + at : INNER + at + 128]
        value = proj_ref[:, 2 * INNER + at : 2 * INNER + at + 128]
        parts = []
        for side in range(2):
            mine = low if side == 0 else jnp.logical_not(low)
            scores = dot_t(pick(mine, query), key) * HEAD_DIM ** (-0.5)
            scores = jnp.where(same_patch, scores, -1e30)
            weights = jnp.exp(scores - jnp.max(scores, -1, keepdims=True))
            probs = weights / jnp.sum(weights, -1, keepdims=True)
            probs_ref[2 * pair + side] = probs
            parts.append(dot(probs.astype(BF16), value))
        results[5 + pair].start()
        attended.append(jnp.where(low, parts[0], parts[1]).astype(BF16))
    wait_all(out_copies)
    hidden = embedded + dot(jnp.concatenate(attended, 1), out_w[...].reshape(INNER, D))
    second, second_scale = normalize(hidden)
    second_ref[...] = second
    second_scale_ref[...] = jnp.broadcast_to(second_scale, (ROWS, 128))
    start_all(results[3:5])
    column = jnp.sum(second * head_ref[0:1, :], -1, keepdims=True)
    on_diagonal = iota((ROWS, ROWS), 0) == iota((ROWS, ROWS), 1)
    line = jnp.sum(jnp.where(on_diagonal, column, 0.0), 0, keepdims=True)
    sums_ref[...] = jnp.broadcast_to(line, (64, ROWS))
    wait_all(results)


def before_kernel(
    second_ref,
    second_scale_ref,
    head_ref,
    proj_ref,
    probs_ref,
    packed_ref,
    hidden_ref,
    attended_ref,
    scores_ref,
    probs_t_ref,
    query_part_ref,
    out_w,
    query_w,
    out_sems,
    query_sems,
):
    out_copies = weight_copies(
        packed_ref, out_sems, [(OUT_AT, 32, 0, D, lambda part: out_w.at[part])]
    )
    query_copies = weight_copies(
        packed_ref, query_sems, [(QKV_AT, 64, 0, INNER, lambda part: query_w.at[part])]
    )
    start_all(out_copies + query_copies)
    second = second_ref[...]
    direction = head_ref[0:1, :] / PATCHES
    hidden = norm_back(direction, second, second_scale_ref[:, 0:1])
    hidden_ref[...] = hidden
    wait_all(out_copies)
    grad_attended = dot_t(hidden.astype(BF16), out_w[...].reshape(INNER, D))
    attended_ref[...] = grad_attended
    low = half_mask()
    grad_query = []
    for pair in range(HEADS // 2):
        at = pair * 2 * HEAD_DIM
        key = proj_ref[:, INNER + at : INNER + at + 128]
        value = proj_ref[:, 2 * INNER + at : 2 * INNER + at + 128]
        grad = grad_attended[:, at : at + 128]
        parts = []
        for side in range(2):
            mine = low if side == 0 else jnp.logical_not(low)
            grad_probs = dot_t(pick(mine, grad), value)
            probs = probs_ref[2 * pair + side]
            delta = jnp.sum(probs * grad_probs, -1, keepdims=True)
            scores = probs * (grad_probs - delta) * HEAD_DIM ** (-0.5)
            parts.append(dot(scores.astype(BF16), key))
            scores_ref[2 * pair + side] = scores.T
            probs_t_ref[2 * pair + side] = probs.T.astype(BF16)
        grad_query.append(jnp.where(low, parts[0], parts[1]).astype(BF16))
    wait_all(query_copies)
    query_part_ref[...] = dot_t(jnp.concatenate(grad_query, 1), query_w[...].reshape(D, INNER))


def backward_kernel(
    everyone_ref,
    scores_in,
    attended_in,
    hidden_in,
    proj_in,
    probs_t_in,
    query_part_in,
    normed_in,
    scale_in,
    packed_ref,
    grad_ref,
    rewards_ref,
    scores_ref,
    attended_ref,
    hidden_ref,
    proj_ref,
    probs_t_ref,
    query_part_ref,
    normed_ref,
    scale_ref,
    grad_proj,
    rest_w,
    patch_w,
    rest_sems,
    patch_sems,
    in_sems,
):
    arrivals = [
        pltpu.make_async_copy(source, target, in_sems.at[i])
        for i, (source, target) in enumerate(
            [
                (scores_in, scores_ref),
                (proj_in.at[:, 0:INNER], proj_ref),
                (probs_t_in, probs_t_ref),
                (attended_in, attended_ref),
                (query_part_in, query_part_ref),
                (normed_in, normed_ref),
                (scale_in, scale_ref),
                (hidden_in, hidden_ref),
            ]
        )
    ]
    rest_copies = weight_copies(packed_ref, rest_sems, qkv_moves(rest_w, INNER, 3 * INNER))
    patch_copies = weight_copies(
        packed_ref, patch_sems, [(PATCH_AT, 48, 0, D, lambda part: patch_w.at[part])]
    )
    start_all(arrivals[0:4] + rest_copies + arrivals[4:] + patch_copies)
    total = jnp.sum(everyone_ref[...], 0, keepdims=True)
    same_frame = (iota((ROWS, ROWS), 0) & 63) == (iota((ROWS, ROWS), 1) & 63)
    rewards = jnp.sum(jnp.where(same_frame, total, 0.0), 1, keepdims=True) / PATCHES
    on_diagonal = iota((ROWS, ROWS), 0) == iota((ROWS, ROWS), 1)
    line = jnp.sum(jnp.where(on_diagonal, rewards, 0.0), 0, keepdims=True)
    factor = -LOSS_SCALE / (1.0 + jnp.exp(rewards))
    factor_line = -LOSS_SCALE / (1.0 + jnp.exp(line))
    rewards_ref[...] = jnp.broadcast_to(line, (8, ROWS))
    low = half_mask()
    wait_all(arrivals[0:4])
    for pair in range(HEADS // 2):
        at = pair * 2 * HEAD_DIM
        query = proj_ref[:, at : at + 128]
        grad = (factor * attended_ref[:, at : at + 128]).astype(BF16)
        parts = []
        for side in range(2):
            scores = (factor_line * scores_ref[2 * pair + side]).astype(BF16)
            parts.append((dot(scores, query), dot(probs_t_ref[2 * pair + side], grad)))
        for part in range(2):
            grad_proj[:, part * INNER + at : part * INNER + at + 128] = jnp.where(
                low, parts[0][part], parts[1][part]
            ).astype(BF16)
    wait_all(rest_copies + arrivals[4:])
    grad_first = factor * query_part_ref[...] + dot_t(
        grad_proj[...], rest_w[...].reshape(D, 2 * INNER)
    )
    grad_embed = norm_back(grad_first, normed_ref[...], scale_ref[:, 0:1]).astype(BF16)
    grad_total = (factor * hidden_ref[...] + grad_embed.astype(F32)).astype(BF16)
    wait_all(patch_copies)
    grad = dot_t(patch_w[...].reshape(PDIM, D), grad_total).astype(BF16)
    for block in range(PDIM // PATCH):
        colour, row = block // PATCH, block % PATCH
        at = ((row // 2) * 6 + (row % 2) * 3 + colour) * PATCH
        grad_ref[at : at + PATCH] = grad[block * PATCH : (block + 1) * PATCH]


def conv_kernel(rows_ref, kernel_ref, out_ref):
    kernel = kernel_ref[...]
    lane = iota((16, IMAGE_W), 1)
    for first in range(0, rows_ref.shape[0], TOGETHER):
        taps = []
        for frame in range(first, first + TOGETHER):
            rows = rows_ref[frame].astype(F32)
            right = jnp.where(lane == IMAGE_W - 1, 0.0, pltpu.roll(rows, IMAGE_W - 1, 1))
            left = jnp.where(lane == 0, 0.0, pltpu.roll(rows, 1, 1))
            taps += [right.astype(BF16), rows_ref[frame], left.astype(BF16)]
        result = dot(kernel, jnp.concatenate(taps, 0)).astype(BF16)
        for frame in range(TOGETHER):
            for row in range(2):
                at = (frame * 2 + row) * 48
                out_ref[first + frame, row] = result[at : at + 48]


def shape(dims, dtype):
    return jax.ShapeDtypeStruct(dims, dtype)


def vmem(count):
    return [pl.BlockSpec(memory_space=pltpu.VMEM)] * count


ANYWHERE = pl.BlockSpec(memory_space=pl.ANY)


def to_patch_rows(pixels):
    frame_count, row_count, _, col_count = pixels.shape
    blocks = pixels.reshape(frame_count, row_count // PATCH, PATCH, 3, col_count // PATCH, PATCH)
    blocks = blocks.transpose(0, 1, 4, 3, 2, 5)
    return blocks.reshape(frame_count, row_count // PATCH * (col_count // PATCH), 3 * PATCH * PATCH)


def conv_matrix(conv_weight):
    flipped = conv_weight[::-1]
    per_row = jnp.stack(
        [jnp.pad(flipped, ((y, 1 - y), (0, 0), (0, 0), (0, 0))) for y in range(2)], 0
    )
    per_row = jnp.pad(per_row, ((0, 0), (0, 0), (0, 0), (0, 0), (0, 1)))
    matrix = per_row.transpose(0, 3, 2, 1, 4).reshape(-1, 48)
    zero = jnp.zeros_like(matrix)
    return jnp.concatenate(
        [
            jnp.concatenate([matrix if i == j else zero for j in range(TOGETHER)], 1)
            for i in range(TOGETHER)
        ],
        0,
    )


def gather_weights(patch_weight, qkv_weight, out_weight):
    half = out_weight.shape[1] // 2
    packed = jnp.concatenate(
        [
            jnp.pad(patch_weight, ((0, SLOT - patch_weight.shape[0]), (0, 0))),
            qkv_weight,
            jnp.concatenate([out_weight[:, :half], out_weight[:, half:]], 0),
        ],
        1,
    )
    near = lax.all_gather(packed, ROW, axis=0)
    core = lax.axis_index("core").astype(jnp.int32).reshape(1)
    return pl.pallas_call(
        arrange_kernel,
        out_shape=shape((BLOCK, D), BF16),
        in_specs=[pl.BlockSpec(memory_space=pltpu.SMEM)] + vmem(1),
        out_specs=vmem(1)[0],
        compiler_params=pltpu.CompilerParams(vmem_limit_bytes=8 * MIB),
        name="arrange",
    )(core, near)


def on_device(pixels, patch_weight, qkv_weight, out_weight, reward_head, conv_weight):
    near = gather_weights(patch_weight, qkv_weight, out_weight)
    near, pixels, conv_weight = lax.optimization_barrier((near, pixels, conv_weight))
    packed = lax.all_gather(near, ("y", "core"), axis=0)
    patches = to_patch_rows(pixels)
    spread = lax.all_to_all(patches, TILE, split_axis=1, concat_axis=0, tiled=True)
    head = jnp.broadcast_to(reward_head[None], (8, D))
    spread, matrix, head = lax.optimization_barrier((spread, conv_matrix(conv_weight), head))
    ordered = pl.pallas_call(
        spread_kernel,
        out_shape=shape((ROWS, PDIM), BF16),
        compiler_params=pltpu.CompilerParams(vmem_limit_bytes=8 * MIB),
        name="spread",
    )(spread.reshape(ROWS, PDIM))
    normed, scale, proj, probs, second, second_scale, sums = pl.pallas_call(
        forward_kernel,
        out_shape=(
            shape((ROWS, D), F32),
            shape((ROWS, 128), F32),
            shape((ROWS, 3 * INNER), BF16),
            shape((HEADS, ROWS, ROWS), F32),
            shape((ROWS, D), F32),
            shape((ROWS, 128), F32),
            shape((64, ROWS), F32),
        ),
        in_specs=vmem(1) + [ANYWHERE] + vmem(1),
        out_specs=tuple([ANYWHERE] * 6 + vmem(1)),
        scratch_shapes=[
            pltpu.VMEM((16, 48, D), BF16),
            pltpu.VMEM((16, 64, 3 * INNER), BF16),
            pltpu.VMEM((16, 32, D), BF16),
            pltpu.VMEM((ROWS, D), F32),
            pltpu.VMEM((ROWS, 128), F32),
            pltpu.VMEM((ROWS, 3 * INNER), BF16),
            pltpu.VMEM((HEADS, ROWS, ROWS), F32),
            pltpu.VMEM((ROWS, D), F32),
            pltpu.VMEM((ROWS, 128), F32),
            pltpu.SemaphoreType.DMA((4,)),
            pltpu.SemaphoreType.DMA((12,)),
            pltpu.SemaphoreType.DMA((4,)),
            pltpu.SemaphoreType.DMA((9,)),
        ],
        name="forward",
    )(ordered, packed, head)
    everyone = lax.all_to_all(sums, TILE, split_axis=0, concat_axis=0, tiled=True)
    hidden, attended, scores, probs_t, query_part = pl.pallas_call(
        before_kernel,
        out_shape=(
            shape((ROWS, D), F32),
            shape((ROWS, INNER), F32),
            shape((HEADS, ROWS, ROWS), F32),
            shape((HEADS, ROWS, ROWS), BF16),
            shape((ROWS, D), F32),
        ),
        in_specs=vmem(5) + [ANYWHERE],
        out_specs=tuple(vmem(5)),
        scratch_shapes=[
            pltpu.VMEM((16, 32, D), BF16),
            pltpu.VMEM((16, 64, INNER), BF16),
            pltpu.SemaphoreType.DMA((4,)),
            pltpu.SemaphoreType.DMA((4,)),
        ],
        cost_estimate=pl.CostEstimate(flops=2**30, transcendentals=0, bytes_accessed=2**23),
        name="before",
    )(second, second_scale, head, proj, probs, packed)
    grad, rewards = pl.pallas_call(
        backward_kernel,
        out_shape=(shape((PDIM, ROWS), BF16), shape((8, ROWS), F32)),
        in_specs=vmem(1) + [ANYWHERE] * 9,
        out_specs=tuple(vmem(2)),
        scratch_shapes=[
            pltpu.VMEM((HEADS, ROWS, ROWS), F32),
            pltpu.VMEM((ROWS, INNER), F32),
            pltpu.VMEM((ROWS, D), F32),
            pltpu.VMEM((ROWS, INNER), BF16),
            pltpu.VMEM((HEADS, ROWS, ROWS), BF16),
            pltpu.VMEM((ROWS, D), F32),
            pltpu.VMEM((ROWS, D), F32),
            pltpu.VMEM((ROWS, 128), F32),
            pltpu.VMEM((ROWS, 2 * INNER), BF16),
            pltpu.VMEM((16, 64, 2 * INNER), BF16),
            pltpu.VMEM((16, 48, D), BF16),
            pltpu.SemaphoreType.DMA((12,)),
            pltpu.SemaphoreType.DMA((4,)),
            pltpu.SemaphoreType.DMA((8,)),
        ],
        name="backward",
    )(
        everyone, scores, attended, hidden, proj, probs_t, query_part, normed, scale, packed
    )
    row_grad = lax.all_to_all(
        grad.reshape(8, PDIM // 8, ROWS), ROW, split_axis=0, concat_axis=0, tiled=True
    )
    row_grad = row_grad.reshape(8, 2, 3 * PATCH, ROWS)
    devices = lax.axis_size(TILE)
    up = [(i, i + 1) for i in range(devices - 1)]
    down = [(i + 1, i) for i in range(devices - 1)]
    before = lax.ppermute(row_grad[:, 1], TILE, up)
    after = lax.ppermute(row_grad[:, 0], TILE, down)
    rows = jnp.concatenate([before[:, None], row_grad, after[:, None]], 1)
    rows = jnp.pad(rows, ((0, 0), (0, 0), (0, PATCH), (0, 0)))
    rows = rows.reshape(8, 4, 4, PATCH, 2, FRAMES).transpose(5, 1, 2, 0, 4, 3)
    rows = rows.reshape(FRAMES, 16, IMAGE_W)
    step = 16
    act_grad = pl.pallas_call(
        conv_kernel,
        out_shape=shape((FRAMES, 2, 48, IMAGE_W), BF16),
        grid=(FRAMES // step,),
        in_specs=[
            pl.BlockSpec((step, 16, IMAGE_W), lambda i: (i, 0, 0)),
            pl.BlockSpec((96 * TOGETHER, 48 * TOGETHER), lambda i: (0, 0)),
        ],
        out_specs=pl.BlockSpec((step, 2, 48, IMAGE_W), lambda i: (i, 0, 0, 0)),
        compiler_params=pltpu.CompilerParams(vmem_limit_bytes=8 * MIB),
        name="conv",
    )(rows, matrix)
    mine = lax.dynamic_slice_in_dim(rewards[0], lax.axis_index(TILE), 1)
    return (mine, act_grad)


def solution(mesh):
    axes = Mesh(mesh.devices.reshape(-1, 4, 8, 4, 2), GRP + TILE)
    in_specs = (
        P(GRP + TILE, None, None, None),
        P(TILE, None),
        P(TILE, None),
        P(TILE, None),
        P(),
        P(),
    )
    out_specs = (P(GRP + TILE), P(GRP, TILE, None, None))
    return jax.shard_map(
        on_device, mesh=axes, in_specs=in_specs, out_specs=out_specs, check_vma=False
    )
```

```python
import jax
import jax.numpy as jnp
from jax import lax
from jax.experimental import pallas as pl
from jax.experimental.pallas import tpu as pltpu
from jax.sharding import Mesh
from jax.sharding import PartitionSpec as P

D = 1024
HEADS = 8
HEAD_DIM = 64
PATCH = 16
PDIM = 768
INNER = HEADS * HEAD_DIM
SLOT = 16
SHARE = 12
PATCH_AT, QKV_AT, TAIL_AT, OUT_AT, BLOCK = 0, 48, 112, 144, 176
FRAMES = 64
PATCHES = 128
ROWS = 128
IMAGE_W = 256
TOGETHER = 4
MIB = 2**20
CHUNKS = 4

GRP = ("zl", "x")
TILE = ("y", "zh", "core")
ROW = ("zh", "core")

LOSS_SCALE = 1024.0
NORM_EPSILON = 1e-05
F32 = jnp.float32
BF16 = jnp.bfloat16


def iota(shape, dim):
    return lax.broadcasted_iota(jnp.int32, shape, dim)


def dot(a, b):
    return lax.dot_general(a, b, (((1,), (0,)), ((), ())), preferred_element_type=F32)


def dot_t(a, b):
    return lax.dot_general(a, b, (((1,), (1,)), ((), ())), preferred_element_type=F32)


def one_hot(condition):
    return jnp.where(condition, 1.0, 0.0).astype(F32).astype(BF16)


def normalize(values_in):
    centred = values_in - jnp.mean(values_in, -1, keepdims=True)
    inverse_scale = lax.rsqrt(jnp.mean(centred * centred, -1, keepdims=True) + NORM_EPSILON)
    return centred * inverse_scale, inverse_scale


def norm_back(grad_in, normed, inverse_scale):
    return inverse_scale * (
        grad_in
        - jnp.mean(grad_in, -1, keepdims=True)
        - normed * jnp.mean(grad_in * normed, -1, keepdims=True)
    )


def weight_copies(packed, sems, moves):
    copies = []
    for row, rows, column, columns, target in moves:
        for part in range(CHUNKS):
            mine = slice(part * 16 // CHUNKS, (part + 1) * 16 // CHUNKS)
            copies.append(
                pltpu.make_async_copy(
                    packed.at[mine, row : row + rows, column : column + columns],
                    target(mine),
                    sems.at[len(copies)],
                )
            )
    return copies


def qkv_moves(target, low, high):
    head, tail = D - low, high - D
    return [
        (QKV_AT, 64, low, head, lambda part: target.at[part, :, 0:head]),
        (TAIL_AT, 32, 0, tail, lambda part: target.at[part, 0:32, head : head + tail]),
        (TAIL_AT, 32, tail, tail, lambda part: target.at[part, 32:64, head : head + tail]),
    ]


def start_all(copies):
    for copy in copies:
        copy.start()


def wait_all(copies):
    for copy in copies:
        copy.wait()


def arrange_kernel(core_ref, near_ref, out_ref):
    slots = near_ref[pl.ds(4 * core_ref[0], 4)].reshape(4 * SLOT, 3 * D)
    slot = iota((48, 4 * SLOT), 1)
    row = jnp.where((slot & 15) < SHARE, SHARE * (slot >> 4) + (slot & 15), -1)
    take = one_hot(row == iota((48, 4 * SLOT), 0))
    out_ref[PATCH_AT:QKV_AT] = dot(take, slots[:, 0:D]).astype(BF16)
    out_ref[QKV_AT:TAIL_AT] = slots[:, D : 2 * D]
    out_ref[TAIL_AT:OUT_AT, 0:INNER] = slots[0:32, 2 * D : 2 * D + INNER]
    out_ref[TAIL_AT:OUT_AT, INNER:D] = slots[32:64, 2 * D : 2 * D + INNER]
    slot = iota((32, 4 * SLOT), 1)
    for half in range(2):
        row = jnp.where(((slot >> 3) & 1) == half, 8 * (slot >> 4) + (slot & 7), -1)
        take = one_hot(row == iota((32, 4 * SLOT), 0))
        out_ref[OUT_AT:BLOCK, half * INNER : (half + 1) * INNER] = dot(
            take, slots[:, 2 * D + INNER : 3 * D]
        ).astype(BF16)


def spread_kernel(patches_ref, out_ref):
    to_row = iota((ROWS, ROWS), 0)
    order = one_hot(iota((ROWS, ROWS), 1) == 2 * (to_row & (FRAMES - 1)) + (to_row >> 6))
    out_ref[...] = dot(order, patches_ref[...]).astype(BF16)


def half_mask():
    return iota((ROWS, 2 * HEAD_DIM), 1) < HEAD_DIM


def pick(condition, value):
    return jnp.where(condition, value.astype(F32), 0.0).astype(BF16)


def forward_kernel(
    patches_ref,
    packed_ref,
    head_ref,
    normed_out,
    scale_out,
    proj_out,
    probs_out,
    second_out,
    second_scale_out,
    sums_out,
    patch_w,
    qkv_w,
    out_w,
    normed_ref,
    scale_ref,
    proj_ref,
    probs_ref,
    second_ref,
    second_scale_ref,
    sums_ref,
    patch_sems,
    qkv_sems,
    weight_sems,
    out_sems,
):
    results = [
        pltpu.make_async_copy(source, target, out_sems.at[i])
        for i, (source, target) in enumerate(
            [
                (normed_ref, normed_out),
                (scale_ref, scale_out),
                (proj_ref, proj_out),
                (second_ref, second_out),
                (second_scale_ref, second_scale_out),
            ]
            + [(probs_ref.at[2 * i : 2 * i + 2], probs_out.at[2 * i : 2 * i + 2]) for i in range(4)]
            + [(sums_ref, sums_out)]
        )
    ]
    patch_copies = weight_copies(
        packed_ref, patch_sems, [(PATCH_AT, 48, 0, D, lambda part: patch_w.at[part])]
    )
    qkv_copies = weight_copies(packed_ref, qkv_sems, qkv_moves(qkv_w, 0, 3 * INNER))
    out_copies = weight_copies(
        packed_ref, weight_sems, [(OUT_AT, 32, 0, D, lambda part: out_w.at[part])]
    )
    start_all(patch_copies + qkv_copies + out_copies)
    wait_all(patch_copies)
    embedded = dot(patches_ref[...], patch_w[...].reshape(PDIM, D)).astype(BF16).astype(F32)
    normed, scale = normalize(embedded)
    normed_ref[...] = normed
    scale_ref[...] = jnp.broadcast_to(scale, (ROWS, 128))
    start_all(results[0:2])
    wait_all(qkv_copies)
    proj_ref[...] = dot(normed.astype(BF16), qkv_w[...].reshape(D, 3 * INNER)).astype(BF16)
    start_all(results[2:3])
    same_patch = (iota((ROWS, ROWS), 0) >> 6) == (iota((ROWS, ROWS), 1) >> 6)
    low = half_mask()
    attended = []
    for pair in range(HEADS // 2):
        at = pair * 2 * HEAD_DIM
        query = proj_ref[:, at : at + 128]
        key = proj_ref[:, INNER + at : INNER + at + 128]
        value = proj_ref[:, 2 * INNER + at : 2 * INNER + at + 128]
        parts = []
        for side in range(2):
            mine = low if side == 0 else jnp.logical_not(low)
            scores = dot_t(pick(mine, query), key) * HEAD_DIM ** (-0.5)
            scores = jnp.where(same_patch, scores, -1e30)
            weights = jnp.exp(scores - jnp.max(scores, -1, keepdims=True))
            probs = weights / jnp.sum(weights, -1, keepdims=True)
            probs_ref[2 * pair + side] = probs
            parts.append(dot(probs.astype(BF16), value))
        results[5 + pair].start()
        attended.append(jnp.where(low, parts[0], parts[1]).astype(BF16))
    wait_all(out_copies)
    hidden = embedded + dot(jnp.concatenate(attended, 1), out_w[...].reshape(INNER, D))
    second, second_scale = normalize(hidden)
    second_ref[...] = second
    second_scale_ref[...] = jnp.broadcast_to(second_scale, (ROWS, 128))
    start_all(results[3:5])
    column = jnp.sum(second * head_ref[0:1, :], -1, keepdims=True)
    on_diagonal = iota((ROWS, ROWS), 0) == iota((ROWS, ROWS), 1)
    line = jnp.sum(jnp.where(on_diagonal, column, 0.0), 0, keepdims=True)
    sums_ref[...] = jnp.broadcast_to(line, (64, ROWS))
    start_all(results[9:])
    wait_all(results)


def before_kernel(
    second_in,
    second_scale_ref,
    head_ref,
    proj_in,
    probs_in,
    packed_ref,
    hidden_out,
    attended_out,
    scores_out,
    probs_t_out,
    query_part_out,
    second_ref,
    proj_ref,
    probs_ref,
    hidden_ref,
    attended_ref,
    scores_ref,
    probs_t_ref,
    query_part_ref,
    out_w,
    query_w,
    out_sems,
    query_sems,
    in_sems,
    result_sems,
):
    arrivals = [
        pltpu.make_async_copy(source, target, in_sems.at[i])
        for i, (source, target) in enumerate(
            [(second_in, second_ref), (proj_in, proj_ref), (probs_in, probs_ref)]
        )
    ]
    results = [
        pltpu.make_async_copy(source, target, result_sems.at[i])
        for i, (source, target) in enumerate(
            [
                (hidden_ref, hidden_out),
                (attended_ref, attended_out),
                (scores_ref, scores_out),
                (probs_t_ref, probs_t_out),
                (query_part_ref, query_part_out),
            ]
        )
    ]
    out_copies = weight_copies(
        packed_ref, out_sems, [(OUT_AT, 32, 0, D, lambda part: out_w.at[part])]
    )
    query_copies = weight_copies(
        packed_ref, query_sems, [(QKV_AT, 64, 0, INNER, lambda part: query_w.at[part])]
    )
    start_all(arrivals)
    start_all(out_copies + query_copies)
    arrivals[0].wait()
    second = second_ref[...]
    direction = head_ref[0:1, :] / PATCHES
    hidden = norm_back(direction, second, second_scale_ref[:, 0:1])
    hidden_ref[...] = hidden
    results[0].start()
    wait_all(out_copies)
    grad_attended = dot_t(hidden.astype(BF16), out_w[...].reshape(INNER, D))
    attended_ref[...] = grad_attended
    results[1].start()
    wait_all(arrivals[1:])
    low = half_mask()
    grad_query = []
    for pair in range(HEADS // 2):
        at = pair * 2 * HEAD_DIM
        key = proj_ref[:, INNER + at : INNER + at + 128]
        value = proj_ref[:, 2 * INNER + at : 2 * INNER + at + 128]
        grad = grad_attended[:, at : at + 128]
        parts = []
        for side in range(2):
            mine = low if side == 0 else jnp.logical_not(low)
            grad_probs = dot_t(pick(mine, grad), value)
            probs = probs_ref[2 * pair + side]
            delta = jnp.sum(probs * grad_probs, -1, keepdims=True)
            scores = probs * (grad_probs - delta) * HEAD_DIM ** (-0.5)
            parts.append(dot(scores.astype(BF16), key))
            scores_ref[2 * pair + side] = scores.T
            probs_t_ref[2 * pair + side] = probs.T.astype(BF16)
        grad_query.append(jnp.where(low, parts[0], parts[1]).astype(BF16))
    start_all(results[2:4])
    wait_all(query_copies)
    query_part_ref[...] = dot_t(jnp.concatenate(grad_query, 1), query_w[...].reshape(D, INNER))
    results[4].start()
    wait_all(results)


def backward_kernel(
    tile_ref,
    everyone_in,
    scores_in,
    attended_in,
    hidden_in,
    proj_in,
    probs_t_in,
    query_part_in,
    normed_in,
    scale_in,
    packed_ref,
    grad_ref,
    rewards_ref,
    scores_ref,
    attended_ref,
    hidden_ref,
    proj_ref,
    probs_t_ref,
    query_part_ref,
    normed_ref,
    scale_ref,
    grad_proj,
    rest_w,
    patch_w,
    rest_sems,
    patch_sems,
    in_sems,
    everyone_ref,
):
    arrivals = [
        pltpu.make_async_copy(source, target, in_sems.at[i])
        for i, (source, target) in enumerate(
            [
                (scores_in, scores_ref),
                (proj_in.at[:, 0:INNER], proj_ref),
                (probs_t_in, probs_t_ref),
                (attended_in, attended_ref),
                (query_part_in, query_part_ref),
                (normed_in, normed_ref),
                (scale_in, scale_ref),
                (hidden_in, hidden_ref),
                (everyone_in, everyone_ref),
            ]
        )
    ]
    rest_copies = weight_copies(packed_ref, rest_sems, qkv_moves(rest_w, INNER, 3 * INNER))
    patch_copies = weight_copies(
        packed_ref, patch_sems, [(PATCH_AT, 48, 0, D, lambda part: patch_w.at[part])]
    )
    start_all(arrivals[8:] + arrivals[0:4] + rest_copies + arrivals[4:8] + patch_copies)
    arrivals[8].wait()
    total = jnp.sum(everyone_ref[...], 0, keepdims=True)
    same_frame = (iota((ROWS, ROWS), 0) & 63) == (iota((ROWS, ROWS), 1) & 63)
    rewards = jnp.sum(jnp.where(same_frame, total, 0.0), 1, keepdims=True) / PATCHES
    on_diagonal = iota((ROWS, ROWS), 0) == iota((ROWS, ROWS), 1)
    line = jnp.sum(jnp.where(on_diagonal, rewards, 0.0), 0, keepdims=True)
    factor = -LOSS_SCALE / (1.0 + jnp.exp(rewards))
    factor_line = -LOSS_SCALE / (1.0 + jnp.exp(line))
    rewards_ref[0] = jnp.sum(jnp.where(iota((1, ROWS), 1) == tile_ref[0], line, 0.0))
    low = half_mask()
    wait_all(arrivals[0:4])
    for pair in range(HEADS // 2):
        at = pair * 2 * HEAD_DIM
        query = proj_ref[:, at : at + 128]
        grad = (factor * attended_ref[:, at : at + 128]).astype(BF16)
        parts = []
        for side in range(2):
            scores = (factor_line * scores_ref[2 * pair + side]).astype(BF16)
            parts.append((dot(scores, query), dot(probs_t_ref[2 * pair + side], grad)))
        for part in range(2):
            grad_proj[:, part * INNER + at : part * INNER + at + 128] = jnp.where(
                low, parts[0][part], parts[1][part]
            ).astype(BF16)
    wait_all(rest_copies + arrivals[4:8])
    grad_first = factor * query_part_ref[...] + dot_t(
        grad_proj[...], rest_w[...].reshape(D, 2 * INNER)
    )
    grad_embed = norm_back(grad_first, normed_ref[...], scale_ref[:, 0:1]).astype(BF16)
    grad_total = (factor * hidden_ref[...] + grad_embed.astype(F32)).astype(BF16)
    wait_all(patch_copies)
    grad = dot_t(patch_w[...].reshape(PDIM, D), grad_total).astype(BF16)
    for block in range(PDIM // PATCH):
        colour, row = block // PATCH, block % PATCH
        at = ((row // 2) * 6 + (row % 2) * 3 + colour) * PATCH
        grad_ref[at : at + PATCH] = grad[block * PATCH : (block + 1) * PATCH]


def conv_kernel(own_ref, halo_ref, kernel_ref, out_ref):
    kernel = kernel_ref[...]
    lane = iota((16, IMAGE_W), 1)
    for first in range(0, own_ref.shape[0], TOGETHER):
        taps = []
        for frame in range(first, first + TOGETHER):
            rows = jnp.concatenate([own_ref[frame].astype(F32), halo_ref[frame].astype(F32)], 0)
            right = jnp.where(lane == IMAGE_W - 1, 0.0, pltpu.roll(rows, IMAGE_W - 1, 1))
            left = jnp.where(lane == 0, 0.0, pltpu.roll(rows, 1, 1))
            taps += [right.astype(BF16), rows.astype(BF16), left.astype(BF16)]
        result = dot(kernel, jnp.concatenate(taps, 0)).astype(BF16)
        for frame in range(TOGETHER):
            for row in range(2):
                at = (frame * 2 + row) * 48
                out_ref[first + frame, row] = result[at : at + 48]


def shape(dims, dtype):
    return jax.ShapeDtypeStruct(dims, dtype)


def vmem(count):
    return [pl.BlockSpec(memory_space=pltpu.VMEM)] * count


ANYWHERE = pl.BlockSpec(memory_space=pl.ANY)
SCALARS = pl.BlockSpec(memory_space=pltpu.SMEM)


def to_patch_rows(pixels):
    frame_count, row_count, _, col_count = pixels.shape
    blocks = pixels.reshape(frame_count, row_count // PATCH, PATCH, 3, col_count // PATCH, PATCH)
    blocks = blocks.transpose(0, 1, 4, 3, 2, 5)
    return blocks.reshape(frame_count, row_count // PATCH * (col_count // PATCH), 3 * PATCH * PATCH)


def conv_matrix(conv_weight):
    flipped = conv_weight[::-1]
    per_row = jnp.stack(
        [jnp.pad(flipped, ((y, 1 - y), (0, 0), (0, 0), (0, 0))) for y in range(2)], 0
    )
    per_row = jnp.pad(per_row, ((0, 0), (0, 0), (0, 0), (0, 0), (0, 1)))
    per_row = jnp.concatenate([per_row[:, 1:3], per_row[:, 0:1], per_row[:, 3:4]], 1)
    matrix = per_row.transpose(0, 3, 2, 1, 4).reshape(-1, 48)
    zero = jnp.zeros_like(matrix)
    return jnp.concatenate(
        [
            jnp.concatenate([matrix if i == j else zero for j in range(TOGETHER)], 1)
            for i in range(TOGETHER)
        ],
        0,
    )


def image_rows(received):
    padded = jnp.pad(received, ((0, 0), (0, 0), (0, PATCH), (0, 0)))
    rows = padded.reshape(8, 2, 4, PATCH, 2, FRAMES).transpose(5, 1, 2, 0, 4, 3)
    return rows.reshape(FRAMES, 8, IMAGE_W)


def gather_weights(patch_weight, qkv_weight, out_weight):
    half = out_weight.shape[1] // 2
    packed = jnp.concatenate(
        [
            jnp.pad(patch_weight, ((0, SLOT - patch_weight.shape[0]), (0, 0))),
            qkv_weight,
            jnp.concatenate([out_weight[:, :half], out_weight[:, half:]], 0),
        ],
        1,
    )
    near = lax.all_gather(packed, ROW, axis=0)
    core = lax.axis_index("core").astype(jnp.int32).reshape(1)
    return pl.pallas_call(
        arrange_kernel,
        out_shape=shape((BLOCK, D), BF16),
        in_specs=[SCALARS] + vmem(1),
        out_specs=vmem(1)[0],
        compiler_params=pltpu.CompilerParams(vmem_limit_bytes=8 * MIB),
        name="arrange",
    )(core, near)


def on_device(pixels, patch_weight, qkv_weight, out_weight, reward_head, conv_weight):
    near = gather_weights(patch_weight, qkv_weight, out_weight)
    near, pixels, conv_weight = lax.optimization_barrier((near, pixels, conv_weight))
    packed = lax.all_gather(near, ("y", "core"), axis=0)
    patches = to_patch_rows(pixels)
    spread = lax.all_to_all(patches, TILE, split_axis=1, concat_axis=0, tiled=True)
    head = jnp.broadcast_to(reward_head[None], (8, D))
    spread, matrix, head = lax.optimization_barrier((spread, conv_matrix(conv_weight), head))
    ordered = pl.pallas_call(
        spread_kernel,
        out_shape=shape((ROWS, PDIM), BF16),
        compiler_params=pltpu.CompilerParams(vmem_limit_bytes=8 * MIB),
        name="spread",
    )(spread.reshape(ROWS, PDIM))
    normed, scale, proj, probs, second, second_scale, sums = pl.pallas_call(
        forward_kernel,
        out_shape=(
            shape((ROWS, D), F32),
            shape((ROWS, 128), F32),
            shape((ROWS, 3 * INNER), BF16),
            shape((HEADS, ROWS, ROWS), F32),
            shape((ROWS, D), F32),
            shape((ROWS, 128), F32),
            shape((64, ROWS), F32),
        ),
        in_specs=vmem(1) + [ANYWHERE] + vmem(1),
        out_specs=tuple([ANYWHERE] * 7),
        scratch_shapes=[
            pltpu.VMEM((16, 48, D), BF16),
            pltpu.VMEM((16, 64, 3 * INNER), BF16),
            pltpu.VMEM((16, 32, D), BF16),
            pltpu.VMEM((ROWS, D), F32),
            pltpu.VMEM((ROWS, 128), F32),
            pltpu.VMEM((ROWS, 3 * INNER), BF16),
            pltpu.VMEM((HEADS, ROWS, ROWS), F32),
            pltpu.VMEM((ROWS, D), F32),
            pltpu.VMEM((ROWS, 128), F32),
            pltpu.VMEM((64, ROWS), F32),
            pltpu.SemaphoreType.DMA((CHUNKS,)),
            pltpu.SemaphoreType.DMA((3 * CHUNKS,)),
            pltpu.SemaphoreType.DMA((CHUNKS,)),
            pltpu.SemaphoreType.DMA((10,)),
        ],
        name="forward",
    )(ordered, packed, head)
    everyone = lax.all_to_all(sums, TILE, split_axis=0, concat_axis=0, tiled=True)
    hidden, attended, scores, probs_t, query_part = pl.pallas_call(
        before_kernel,
        out_shape=(
            shape((ROWS, D), F32),
            shape((ROWS, INNER), F32),
            shape((HEADS, ROWS, ROWS), F32),
            shape((HEADS, ROWS, ROWS), BF16),
            shape((ROWS, D), F32),
        ),
        in_specs=[ANYWHERE] + vmem(2) + [ANYWHERE] * 3,
        out_specs=tuple([ANYWHERE] * 5),
        scratch_shapes=[
            pltpu.VMEM((ROWS, D), F32),
            pltpu.VMEM((ROWS, 3 * INNER), BF16),
            pltpu.VMEM((HEADS, ROWS, ROWS), F32),
            pltpu.VMEM((ROWS, D), F32),
            pltpu.VMEM((ROWS, INNER), F32),
            pltpu.VMEM((HEADS, ROWS, ROWS), F32),
            pltpu.VMEM((HEADS, ROWS, ROWS), BF16),
            pltpu.VMEM((ROWS, D), F32),
            pltpu.VMEM((16, 32, D), BF16),
            pltpu.VMEM((16, 64, INNER), BF16),
            pltpu.SemaphoreType.DMA((CHUNKS,)),
            pltpu.SemaphoreType.DMA((CHUNKS,)),
            pltpu.SemaphoreType.DMA((3,)),
            pltpu.SemaphoreType.DMA((5,)),
        ],
        cost_estimate=pl.CostEstimate(flops=2**30, transcendentals=0, bytes_accessed=2**23),
        name="before",
    )(second, second_scale, head, proj, probs, packed)
    tile = lax.axis_index(TILE).astype(jnp.int32).reshape(1)
    grad, rewards = pl.pallas_call(
        backward_kernel,
        out_shape=(shape((PDIM, ROWS), BF16), shape((1,), F32)),
        in_specs=[SCALARS] + [ANYWHERE] * 10,
        out_specs=(vmem(1)[0], SCALARS),
        scratch_shapes=[
            pltpu.VMEM((HEADS, ROWS, ROWS), F32),
            pltpu.VMEM((ROWS, INNER), F32),
            pltpu.VMEM((ROWS, D), F32),
            pltpu.VMEM((ROWS, INNER), BF16),
            pltpu.VMEM((HEADS, ROWS, ROWS), BF16),
            pltpu.VMEM((ROWS, D), F32),
            pltpu.VMEM((ROWS, D), F32),
            pltpu.VMEM((ROWS, 128), F32),
            pltpu.VMEM((ROWS, 2 * INNER), BF16),
            pltpu.VMEM((16, 64, 2 * INNER), BF16),
            pltpu.VMEM((16, 48, D), BF16),
            pltpu.SemaphoreType.DMA((3 * CHUNKS,)),
            pltpu.SemaphoreType.DMA((CHUNKS,)),
            pltpu.SemaphoreType.DMA((9,)),
            pltpu.VMEM((64, ROWS), F32),
        ],
        name="backward",
    )(
        tile, everyone, scores, attended, hidden, proj, probs_t, query_part, normed, scale, packed
    )
    row_grad = lax.all_to_all(
        grad.reshape(8, PDIM // 8, ROWS), ROW, split_axis=0, concat_axis=0, tiled=True
    )
    row_grad = row_grad.reshape(8, 2, 3 * PATCH, ROWS)
    devices = lax.axis_size(TILE)
    up = [(i, i + 1) for i in range(devices - 1)]
    down = [(i + 1, i) for i in range(devices - 1)]
    before = lax.ppermute(row_grad[:, 1], TILE, up)
    after = lax.ppermute(row_grad[:, 0], TILE, down)
    own = image_rows(row_grad)
    halo = image_rows(jnp.stack([before, after], 1))
    step = 16
    act_grad = pl.pallas_call(
        conv_kernel,
        out_shape=shape((FRAMES, 2, 48, IMAGE_W), BF16),
        grid=(FRAMES // step,),
        in_specs=[
            pl.BlockSpec((step, 8, IMAGE_W), lambda i: (i, 0, 0)),
            pl.BlockSpec((step, 8, IMAGE_W), lambda i: (i, 0, 0)),
            pl.BlockSpec((96 * TOGETHER, 48 * TOGETHER), lambda i: (0, 0)),
        ],
        out_specs=pl.BlockSpec((step, 2, 48, IMAGE_W), lambda i: (i, 0, 0, 0)),
        compiler_params=pltpu.CompilerParams(vmem_limit_bytes=8 * MIB),
        name="conv",
    )(own, halo, matrix)
    return (rewards, act_grad)


def solution(mesh):
    axes = Mesh(mesh.devices.reshape(-1, 4, 8, 4, 2), GRP + TILE)
    in_specs = (
        P(GRP + TILE, None, None, None),
        P(TILE, None),
        P(TILE, None),
        P(TILE, None),
        P(),
        P(),
    )
    out_specs = (P(GRP + TILE), P(GRP, TILE, None, None))
    return jax.shard_map(
        on_device, mesh=axes, in_specs=in_specs, out_specs=out_specs, check_vma=False
    )
```

```python
import jax
import jax.numpy as jnp
from jax import lax
from jax.experimental import pallas as pl
from jax.experimental.pallas import tpu as pltpu
from jax.sharding import Mesh
from jax.sharding import PartitionSpec as P

D = 1024
HEADS = 8
HEAD_DIM = 64
PATCH = 16
PDIM = 768
INNER = HEADS * HEAD_DIM
SLOT = 16
SHARE = 12
PATCH_AT, QKV_AT, TAIL_AT, OUT_AT, BLOCK = 0, 48, 112, 144, 176
FRAMES = 64
PATCHES = 128
ROWS = 128
IMAGE_W = 256
TOGETHER = 4
MIB = 2**20
CHUNKS = 2

GRP = ("zl", "x")
TILE = ("y", "zh", "core")
ROW = ("zh", "core")

LOSS_SCALE = 1024.0
NORM_EPSILON = 1e-05
F32 = jnp.float32
BF16 = jnp.bfloat16


def iota(shape, dim):
    return lax.broadcasted_iota(jnp.int32, shape, dim)


def dot(a, b):
    return lax.dot_general(a, b, (((1,), (0,)), ((), ())), preferred_element_type=F32)


def dot_t(a, b):
    return lax.dot_general(a, b, (((1,), (1,)), ((), ())), preferred_element_type=F32)


def one_hot(condition):
    return jnp.where(condition, 1.0, 0.0).astype(F32).astype(BF16)


def normalize(values_in):
    centred = values_in - jnp.mean(values_in, -1, keepdims=True)
    inverse_scale = lax.rsqrt(jnp.mean(centred * centred, -1, keepdims=True) + NORM_EPSILON)
    return centred * inverse_scale, inverse_scale


def norm_back(grad_in, normed, inverse_scale):
    return inverse_scale * (
        grad_in
        - jnp.mean(grad_in, -1, keepdims=True)
        - normed * jnp.mean(grad_in * normed, -1, keepdims=True)
    )


def weight_copies(packed, sems, moves):
    copies = []
    for row, rows, column, columns, target in moves:
        for part in range(CHUNKS):
            mine = slice(part * 16 // CHUNKS, (part + 1) * 16 // CHUNKS)
            copies.append(
                pltpu.make_async_copy(
                    packed.at[mine, row : row + rows, column : column + columns],
                    target(mine),
                    sems.at[len(copies)],
                )
            )
    return copies


def qkv_moves(target, low, high):
    head, tail = D - low, high - D
    return [
        (QKV_AT, 64, low, head, lambda part: target.at[part, :, 0:head]),
        (TAIL_AT, 32, 0, tail, lambda part: target.at[part, 0:32, head : head + tail]),
        (TAIL_AT, 32, tail, tail, lambda part: target.at[part, 32:64, head : head + tail]),
    ]


def start_all(copies):
    for copy in copies:
        copy.start()


def wait_all(copies):
    for copy in copies:
        copy.wait()


def arrange_kernel(core_ref, near_ref, out_ref):
    slots = near_ref[pl.ds(4 * core_ref[0], 4)].reshape(4 * SLOT, 3 * D)
    slot = iota((48, 4 * SLOT), 1)
    row = jnp.where((slot & 15) < SHARE, SHARE * (slot >> 4) + (slot & 15), -1)
    take = one_hot(row == iota((48, 4 * SLOT), 0))
    out_ref[PATCH_AT:QKV_AT] = dot(take, slots[:, 0:D]).astype(BF16)
    out_ref[QKV_AT:TAIL_AT] = slots[:, D : 2 * D]
    out_ref[TAIL_AT:OUT_AT, 0:INNER] = slots[0:32, 2 * D : 2 * D + INNER]
    out_ref[TAIL_AT:OUT_AT, INNER:D] = slots[32:64, 2 * D : 2 * D + INNER]
    slot = iota((32, 4 * SLOT), 1)
    for half in range(2):
        row = jnp.where(((slot >> 3) & 1) == half, 8 * (slot >> 4) + (slot & 7), -1)
        take = one_hot(row == iota((32, 4 * SLOT), 0))
        out_ref[OUT_AT:BLOCK, half * INNER : (half + 1) * INNER] = dot(
            take, slots[:, 2 * D + INNER : 3 * D]
        ).astype(BF16)


def spread_kernel(patches_ref, out_ref):
    to_row = iota((ROWS, ROWS), 0)
    order = one_hot(iota((ROWS, ROWS), 1) == 2 * (to_row & (FRAMES - 1)) + (to_row >> 6))
    out_ref[...] = dot(order, patches_ref[...]).astype(BF16)


def half_mask():
    return iota((ROWS, 2 * HEAD_DIM), 1) < HEAD_DIM


def pick(condition, value):
    return jnp.where(condition, value.astype(F32), 0.0).astype(BF16)


def forward_kernel(
    patches_ref,
    packed_ref,
    head_ref,
    normed_out,
    scale_out,
    proj_out,
    probs_out,
    second_out,
    second_scale_out,
    sums_out,
    patch_w,
    qkv_w,
    out_w,
    normed_ref,
    scale_ref,
    proj_ref,
    probs_ref,
    second_ref,
    second_scale_ref,
    sums_ref,
    patch_sems,
    qkv_sems,
    weight_sems,
    out_sems,
):
    results = [
        pltpu.make_async_copy(source, target, out_sems.at[i])
        for i, (source, target) in enumerate(
            [
                (normed_ref, normed_out),
                (scale_ref, scale_out),
                (proj_ref, proj_out),
                (second_ref, second_out),
                (second_scale_ref, second_scale_out),
            ]
            + [(probs_ref.at[2 * i : 2 * i + 2], probs_out.at[2 * i : 2 * i + 2]) for i in range(4)]
            + [(sums_ref, sums_out)]
        )
    ]
    patch_copies = weight_copies(
        packed_ref, patch_sems, [(PATCH_AT, 48, 0, D, lambda part: patch_w.at[part])]
    )
    qkv_copies = weight_copies(packed_ref, qkv_sems, qkv_moves(qkv_w, 0, 3 * INNER))
    out_copies = weight_copies(
        packed_ref, weight_sems, [(OUT_AT, 32, 0, D, lambda part: out_w.at[part])]
    )
    start_all(patch_copies + qkv_copies + out_copies)
    wait_all(patch_copies)
    embedded = dot(patches_ref[...], patch_w[...].reshape(PDIM, D)).astype(BF16).astype(F32)
    normed, scale = normalize(embedded)
    normed_ref[...] = normed
    scale_ref[...] = jnp.broadcast_to(scale, (ROWS, 128))
    start_all(results[0:2])
    wait_all(qkv_copies)
    proj_ref[...] = dot(normed.astype(BF16), qkv_w[...].reshape(D, 3 * INNER)).astype(BF16)
    start_all(results[2:3])
    same_patch = (iota((ROWS, ROWS), 0) >> 6) == (iota((ROWS, ROWS), 1) >> 6)
    low = half_mask()
    attended = []
    for pair in range(HEADS // 2):
        at = pair * 2 * HEAD_DIM
        query = proj_ref[:, at : at + 128]
        key = proj_ref[:, INNER + at : INNER + at + 128]
        value = proj_ref[:, 2 * INNER + at : 2 * INNER + at + 128]
        parts = []
        for side in range(2):
            mine = low if side == 0 else jnp.logical_not(low)
            scores = dot_t(pick(mine, query), key) * HEAD_DIM ** (-0.5)
            scores = jnp.where(same_patch, scores, -1e30)
            weights = jnp.exp(scores - jnp.max(scores, -1, keepdims=True))
            probs = weights / jnp.sum(weights, -1, keepdims=True)
            probs_ref[2 * pair + side] = probs
            parts.append(dot(probs.astype(BF16), value))
        results[5 + pair].start()
        attended.append(jnp.where(low, parts[0], parts[1]).astype(BF16))
    wait_all(out_copies)
    hidden = embedded + dot(jnp.concatenate(attended, 1), out_w[...].reshape(INNER, D))
    second, second_scale = normalize(hidden)
    second_ref[...] = second
    second_scale_ref[...] = jnp.broadcast_to(second_scale, (ROWS, 128))
    start_all(results[3:5])
    column = jnp.sum(second * head_ref[0:1, :], -1, keepdims=True)
    on_diagonal = iota((ROWS, ROWS), 0) == iota((ROWS, ROWS), 1)
    line = jnp.sum(jnp.where(on_diagonal, column, 0.0), 0, keepdims=True)
    sums_ref[...] = jnp.broadcast_to(line, (64, ROWS))
    start_all(results[9:])
    wait_all(results)


def before_kernel(
    second_in,
    second_scale_ref,
    head_ref,
    proj_in,
    probs_in,
    packed_ref,
    hidden_out,
    attended_out,
    scores_out,
    probs_t_out,
    query_part_out,
    second_ref,
    proj_ref,
    probs_ref,
    hidden_ref,
    attended_ref,
    scores_ref,
    probs_t_ref,
    query_part_ref,
    out_w,
    query_w,
    out_sems,
    query_sems,
    in_sems,
    result_sems,
):
    arrivals = [
        pltpu.make_async_copy(source, target, in_sems.at[i])
        for i, (source, target) in enumerate(
            [(second_in, second_ref), (proj_in, proj_ref), (probs_in, probs_ref)]
        )
    ]
    results = [
        pltpu.make_async_copy(source, target, result_sems.at[i])
        for i, (source, target) in enumerate(
            [
                (hidden_ref, hidden_out),
                (attended_ref, attended_out),
                (scores_ref, scores_out),
                (probs_t_ref, probs_t_out),
                (query_part_ref, query_part_out),
            ]
        )
    ]
    out_copies = weight_copies(
        packed_ref, out_sems, [(OUT_AT, 32, 0, D, lambda part: out_w.at[part])]
    )
    query_copies = weight_copies(
        packed_ref, query_sems, [(QKV_AT, 64, 0, INNER, lambda part: query_w.at[part])]
    )
    start_all(arrivals)
    start_all(out_copies + query_copies)
    arrivals[0].wait()
    second = second_ref[...]
    direction = head_ref[0:1, :] / PATCHES
    hidden = norm_back(direction, second, second_scale_ref[:, 0:1])
    hidden_ref[...] = hidden
    results[0].start()
    wait_all(out_copies)
    grad_attended = dot_t(hidden.astype(BF16), out_w[...].reshape(INNER, D))
    attended_ref[...] = grad_attended
    results[1].start()
    wait_all(arrivals[1:])
    low = half_mask()
    grad_query = []
    for pair in range(HEADS // 2):
        at = pair * 2 * HEAD_DIM
        key = proj_ref[:, INNER + at : INNER + at + 128]
        value = proj_ref[:, 2 * INNER + at : 2 * INNER + at + 128]
        grad = grad_attended[:, at : at + 128]
        parts = []
        for side in range(2):
            mine = low if side == 0 else jnp.logical_not(low)
            grad_probs = dot_t(pick(mine, grad), value)
            probs = probs_ref[2 * pair + side]
            delta = jnp.sum(probs * grad_probs, -1, keepdims=True)
            scores = (probs * (grad_probs - delta) * HEAD_DIM ** (-0.5)).astype(BF16)
            parts.append(dot(scores, key))
            scores_ref[2 * pair + side] = scores.T
            probs_t_ref[2 * pair + side] = probs.astype(BF16).T
        grad_query.append(jnp.where(low, parts[0], parts[1]).astype(BF16))
    start_all(results[2:4])
    wait_all(query_copies)
    query_part_ref[...] = dot_t(jnp.concatenate(grad_query, 1), query_w[...].reshape(D, INNER))
    results[4].start()
    wait_all(results)


def backward_kernel(
    tile_ref,
    everyone_in,
    scores_in,
    attended_in,
    hidden_in,
    proj_in,
    probs_t_in,
    query_part_in,
    normed_in,
    scale_in,
    packed_ref,
    grad_ref,
    rewards_ref,
    scores_ref,
    attended_ref,
    hidden_ref,
    proj_ref,
    probs_t_ref,
    query_part_ref,
    normed_ref,
    scale_ref,
    grad_proj,
    rest_w,
    patch_w,
    rest_sems,
    patch_sems,
    in_sems,
    everyone_ref,
):
    arrivals = [
        pltpu.make_async_copy(source, target, in_sems.at[i])
        for i, (source, target) in enumerate(
            [
                (scores_in, scores_ref),
                (proj_in.at[:, 0:INNER], proj_ref),
                (probs_t_in, probs_t_ref),
                (attended_in, attended_ref),
                (query_part_in, query_part_ref),
                (normed_in, normed_ref),
                (scale_in, scale_ref),
                (hidden_in, hidden_ref),
                (everyone_in, everyone_ref),
            ]
        )
    ]
    rest_copies = weight_copies(packed_ref, rest_sems, qkv_moves(rest_w, INNER, 3 * INNER))
    patch_copies = weight_copies(
        packed_ref, patch_sems, [(PATCH_AT, 48, 0, D, lambda part: patch_w.at[part])]
    )
    start_all(arrivals[8:] + arrivals[0:4] + rest_copies + arrivals[4:8] + patch_copies)
    arrivals[8].wait()
    total = jnp.sum(everyone_ref[...], 0, keepdims=True)
    same_frame = (iota((ROWS, ROWS), 0) & 63) == (iota((ROWS, ROWS), 1) & 63)
    rewards = jnp.sum(jnp.where(same_frame, total, 0.0), 1, keepdims=True) / PATCHES
    on_diagonal = iota((ROWS, ROWS), 0) == iota((ROWS, ROWS), 1)
    line = jnp.sum(jnp.where(on_diagonal, rewards, 0.0), 0, keepdims=True)
    factor = -LOSS_SCALE / (1.0 + jnp.exp(rewards))
    factor_line = -LOSS_SCALE / (1.0 + jnp.exp(line))
    rewards_ref[0] = jnp.sum(jnp.where(iota((1, ROWS), 1) == tile_ref[0], line, 0.0))
    low = half_mask()
    wait_all(arrivals[0:4])
    for pair in range(HEADS // 2):
        at = pair * 2 * HEAD_DIM
        query = proj_ref[:, at : at + 128]
        grad = (factor * attended_ref[:, at : at + 128]).astype(BF16)
        parts = []
        for side in range(2):
            scores = (factor_line * scores_ref[2 * pair + side].astype(F32)).astype(BF16)
            parts.append((dot(scores, query), dot(probs_t_ref[2 * pair + side], grad)))
        for part in range(2):
            grad_proj[:, part * INNER + at : part * INNER + at + 128] = jnp.where(
                low, parts[0][part], parts[1][part]
            ).astype(BF16)
    wait_all(rest_copies + arrivals[4:8])
    grad_first = factor * query_part_ref[...] + dot_t(
        grad_proj[...], rest_w[...].reshape(D, 2 * INNER)
    )
    grad_embed = norm_back(grad_first, normed_ref[...], scale_ref[:, 0:1]).astype(BF16)
    grad_total = (factor * hidden_ref[...] + grad_embed.astype(F32)).astype(BF16)
    wait_all(patch_copies)
    grad = dot_t(patch_w[...].reshape(PDIM, D), grad_total).astype(BF16)
    for block in range(PDIM // PATCH):
        colour, row = block // PATCH, block % PATCH
        at = ((row // 2) * 6 + (row % 2) * 3 + colour) * PATCH
        grad_ref[at : at + PATCH] = grad[block * PATCH : (block + 1) * PATCH]


def conv_kernel(own_ref, halo_ref, kernel_ref, out_ref):
    kernel = kernel_ref[...]
    lane = iota((16, IMAGE_W), 1)
    for first in range(0, own_ref.shape[0], TOGETHER):
        taps = []
        for frame in range(first, first + TOGETHER):
            rows = jnp.concatenate([own_ref[frame].astype(F32), halo_ref[frame].astype(F32)], 0)
            right = jnp.where(lane == IMAGE_W - 1, 0.0, pltpu.roll(rows, IMAGE_W - 1, 1))
            left = jnp.where(lane == 0, 0.0, pltpu.roll(rows, 1, 1))
            taps += [right.astype(BF16), rows.astype(BF16), left.astype(BF16)]
        result = dot(kernel, jnp.concatenate(taps, 0)).astype(BF16)
        for frame in range(TOGETHER):
            for row in range(2):
                at = (frame * 2 + row) * 48
                out_ref[first + frame, row] = result[at : at + 48]


def shape(dims, dtype):
    return jax.ShapeDtypeStruct(dims, dtype)


def vmem(count):
    return [pl.BlockSpec(memory_space=pltpu.VMEM)] * count


ANYWHERE = pl.BlockSpec(memory_space=pl.ANY)
SCALARS = pl.BlockSpec(memory_space=pltpu.SMEM)


def to_patch_rows(pixels):
    frame_count, row_count, _, col_count = pixels.shape
    blocks = pixels.reshape(frame_count, row_count // PATCH, PATCH, 3, col_count // PATCH, PATCH)
    blocks = blocks.transpose(0, 1, 4, 3, 2, 5)
    return blocks.reshape(frame_count, row_count // PATCH * (col_count // PATCH), 3 * PATCH * PATCH)


def conv_matrix(conv_weight):
    flipped = conv_weight[::-1]
    per_row = jnp.stack(
        [jnp.pad(flipped, ((y, 1 - y), (0, 0), (0, 0), (0, 0))) for y in range(2)], 0
    )
    per_row = jnp.pad(per_row, ((0, 0), (0, 0), (0, 0), (0, 0), (0, 1)))
    per_row = jnp.concatenate([per_row[:, 1:3], per_row[:, 0:1], per_row[:, 3:4]], 1)
    matrix = per_row.transpose(0, 3, 2, 1, 4).reshape(-1, 48)
    zero = jnp.zeros_like(matrix)
    return jnp.concatenate(
        [
            jnp.concatenate([matrix if i == j else zero for j in range(TOGETHER)], 1)
            for i in range(TOGETHER)
        ],
        0,
    )


def image_rows(received):
    padded = jnp.pad(received, ((0, 0), (0, 0), (0, PATCH), (0, 0)))
    rows = padded.reshape(8, 2, 4, PATCH, 2, FRAMES).transpose(5, 1, 2, 0, 4, 3)
    return rows.reshape(FRAMES, 8, IMAGE_W)


def gather_weights(patch_weight, qkv_weight, out_weight):
    half = out_weight.shape[1] // 2
    packed = jnp.concatenate(
        [
            jnp.pad(patch_weight, ((0, SLOT - patch_weight.shape[0]), (0, 0))),
            qkv_weight,
            jnp.concatenate([out_weight[:, :half], out_weight[:, half:]], 0),
        ],
        1,
    )
    near = lax.all_gather(packed, ROW, axis=0)
    core = lax.axis_index("core").astype(jnp.int32).reshape(1)
    return pl.pallas_call(
        arrange_kernel,
        out_shape=shape((BLOCK, D), BF16),
        in_specs=[SCALARS] + vmem(1),
        out_specs=vmem(1)[0],
        compiler_params=pltpu.CompilerParams(vmem_limit_bytes=8 * MIB),
        name="arrange",
    )(core, near)


def on_device(pixels, patch_weight, qkv_weight, out_weight, reward_head, conv_weight):
    near = gather_weights(patch_weight, qkv_weight, out_weight)
    near, pixels, conv_weight = lax.optimization_barrier((near, pixels, conv_weight))
    packed = lax.all_gather(near, ("y", "core"), axis=0)
    patches = to_patch_rows(pixels)
    spread = lax.all_to_all(patches, TILE, split_axis=1, concat_axis=0, tiled=True)
    head = jnp.broadcast_to(reward_head[None], (8, D))
    spread, matrix, head = lax.optimization_barrier((spread, conv_matrix(conv_weight), head))
    ordered = pl.pallas_call(
        spread_kernel,
        out_shape=shape((ROWS, PDIM), BF16),
        compiler_params=pltpu.CompilerParams(vmem_limit_bytes=8 * MIB),
        name="spread",
    )(spread.reshape(ROWS, PDIM))
    normed, scale, proj, probs, second, second_scale, sums = pl.pallas_call(
        forward_kernel,
        out_shape=(
            shape((ROWS, D), F32),
            shape((ROWS, 128), F32),
            shape((ROWS, 3 * INNER), BF16),
            shape((HEADS, ROWS, ROWS), F32),
            shape((ROWS, D), F32),
            shape((ROWS, 128), F32),
            shape((64, ROWS), F32),
        ),
        in_specs=vmem(1) + [ANYWHERE] + vmem(1),
        out_specs=tuple([ANYWHERE] * 7),
        scratch_shapes=[
            pltpu.VMEM((16, 48, D), BF16),
            pltpu.VMEM((16, 64, 3 * INNER), BF16),
            pltpu.VMEM((16, 32, D), BF16),
            pltpu.VMEM((ROWS, D), F32),
            pltpu.VMEM((ROWS, 128), F32),
            pltpu.VMEM((ROWS, 3 * INNER), BF16),
            pltpu.VMEM((HEADS, ROWS, ROWS), F32),
            pltpu.VMEM((ROWS, D), F32),
            pltpu.VMEM((ROWS, 128), F32),
            pltpu.VMEM((64, ROWS), F32),
            pltpu.SemaphoreType.DMA((CHUNKS,)),
            pltpu.SemaphoreType.DMA((3 * CHUNKS,)),
            pltpu.SemaphoreType.DMA((CHUNKS,)),
            pltpu.SemaphoreType.DMA((10,)),
        ],
        name="forward",
    )(ordered, packed, head)
    everyone = lax.all_to_all(sums, TILE, split_axis=0, concat_axis=0, tiled=True)
    hidden, attended, scores, probs_t, query_part = pl.pallas_call(
        before_kernel,
        out_shape=(
            shape((ROWS, D), F32),
            shape((ROWS, INNER), F32),
            shape((HEADS, ROWS, ROWS), BF16),
            shape((HEADS, ROWS, ROWS), BF16),
            shape((ROWS, D), F32),
        ),
        in_specs=[ANYWHERE] + vmem(2) + [ANYWHERE] * 3,
        out_specs=tuple([ANYWHERE] * 5),
        scratch_shapes=[
            pltpu.VMEM((ROWS, D), F32),
            pltpu.VMEM((ROWS, 3 * INNER), BF16),
            pltpu.VMEM((HEADS, ROWS, ROWS), F32),
            pltpu.VMEM((ROWS, D), F32),
            pltpu.VMEM((ROWS, INNER), F32),
            pltpu.VMEM((HEADS, ROWS, ROWS), BF16),
            pltpu.VMEM((HEADS, ROWS, ROWS), BF16),
            pltpu.VMEM((ROWS, D), F32),
            pltpu.VMEM((16, 32, D), BF16),
            pltpu.VMEM((16, 64, INNER), BF16),
            pltpu.SemaphoreType.DMA((CHUNKS,)),
            pltpu.SemaphoreType.DMA((CHUNKS,)),
            pltpu.SemaphoreType.DMA((3,)),
            pltpu.SemaphoreType.DMA((5,)),
        ],
        cost_estimate=pl.CostEstimate(flops=2**30, transcendentals=0, bytes_accessed=2**23),
        name="before",
    )(second, second_scale, head, proj, probs, packed)
    tile = lax.axis_index(TILE).astype(jnp.int32).reshape(1)
    grad, rewards = pl.pallas_call(
        backward_kernel,
        out_shape=(shape((PDIM, ROWS), BF16), shape((1,), F32)),
        in_specs=[SCALARS] + [ANYWHERE] * 10,
        out_specs=(vmem(1)[0], SCALARS),
        scratch_shapes=[
            pltpu.VMEM((HEADS, ROWS, ROWS), BF16),
            pltpu.VMEM((ROWS, INNER), F32),
            pltpu.VMEM((ROWS, D), F32),
            pltpu.VMEM((ROWS, INNER), BF16),
            pltpu.VMEM((HEADS, ROWS, ROWS), BF16),
            pltpu.VMEM((ROWS, D), F32),
            pltpu.VMEM((ROWS, D), F32),
            pltpu.VMEM((ROWS, 128), F32),
            pltpu.VMEM((ROWS, 2 * INNER), BF16),
            pltpu.VMEM((16, 64, 2 * INNER), BF16),
            pltpu.VMEM((16, 48, D), BF16),
            pltpu.SemaphoreType.DMA((3 * CHUNKS,)),
            pltpu.SemaphoreType.DMA((CHUNKS,)),
            pltpu.SemaphoreType.DMA((9,)),
            pltpu.VMEM((64, ROWS), F32),
        ],
        name="backward",
    )(
        tile, everyone, scores, attended, hidden, proj, probs_t, query_part, normed, scale, packed
    )
    row_grad = lax.all_to_all(
        grad.reshape(8, PDIM // 8, ROWS), ROW, split_axis=0, concat_axis=0, tiled=True
    )
    row_grad = row_grad.reshape(8, 2, 3 * PATCH, ROWS)
    devices = lax.axis_size(TILE)
    up = [(i, i + 1) for i in range(devices - 1)]
    down = [(i + 1, i) for i in range(devices - 1)]
    before = lax.ppermute(row_grad[:, 1], TILE, up)
    after = lax.ppermute(row_grad[:, 0], TILE, down)
    own = image_rows(row_grad)
    halo = image_rows(jnp.stack([before, after], 1))
    step = 16
    act_grad = pl.pallas_call(
        conv_kernel,
        out_shape=shape((FRAMES, 2, 48, IMAGE_W), BF16),
        grid=(FRAMES // step,),
        in_specs=[
            pl.BlockSpec((step, 8, IMAGE_W), lambda i: (i, 0, 0)),
            pl.BlockSpec((step, 8, IMAGE_W), lambda i: (i, 0, 0)),
            pl.BlockSpec((96 * TOGETHER, 48 * TOGETHER), lambda i: (0, 0)),
        ],
        out_specs=pl.BlockSpec((step, 2, 48, IMAGE_W), lambda i: (i, 0, 0, 0)),
        compiler_params=pltpu.CompilerParams(vmem_limit_bytes=8 * MIB),
        name="conv",
    )(own, halo, matrix)
    return (rewards, act_grad)


def solution(mesh):
    axes = Mesh(mesh.devices.reshape(-1, 4, 8, 4, 2), GRP + TILE)
    in_specs = (
        P(GRP + TILE, None, None, None),
        P(TILE, None),
        P(TILE, None),
        P(TILE, None),
        P(),
        P(),
    )
    out_specs = (P(GRP + TILE), P(GRP, TILE, None, None))
    return jax.shard_map(
        on_device, mesh=axes, in_specs=in_specs, out_specs=out_specs, check_vma=False
    )
```
